256 devices in a mesh: areal: 64 (over x, y, z_hi, core), layer: 4 (over z_lo).
Axes of the slice: x: 4, y: 4, z: 8 (z_hi: 2, z_lo: 4; z = z_hi * 4 + z_lo), core: 2. Of those that a mesh axis runs over, the one named last changes fastest.
Arguments:
- pressure: float32 [8, 2048, 1024], P(None, 'areal', 'layer'), may hold values from 0.7 to 1.4
- composition: float32 [9, 8, 2048, 1024], P(None, None, 'areal', 'layer'), may hold values from 0.02 to 1
- mass_old: float32 [9, 8, 2048, 1024], P(None, None, 'areal', 'layer'), may hold values from 0 to 0.3
- pore_volume: float32 [8, 2048, 1024], P(None, 'areal', 'layer'), may hold values from 0.5 to 2
- trans_x: float32 [8, 2048, 1024], P(None, 'areal', 'layer'), may hold values from 0.3 to 3
- trans_y: float32 [8, 2048, 1024], P(None, 'areal', 'layer'), may hold values from 0.3 to 3
- trans_z: float32 [8, 2048, 1024], P(None, 'areal', 'layer'), may hold values from 0.3 to 3
- volatility: float32 [9], replicated, may hold values from 1.5 to 3
- pressure_slope: float32 [9], replicated, may hold values from 0.2 to 1
- mixing: float32 [9, 9], replicated, may hold values from -3.5 to 3.5
- two_phase: int32 [4, 512], P(None, 'areal'), may hold values from 0 to 1, as said below
Outputs:
- residual: float32 [9, 8, 2048, 1024], P(None, None, 'areal', 'layer')
- new_pressure: float32 [8, 2048, 1024], P(None, 'areal', 'layer')
The draws below stay inside these ranges and needn't reach their ends.
Inputs may be any that keep to these rules, and one draw needn't show every extreme that they name: `two_phase`: for each areal index, the 4 rows together flag exactly 16 of their bricks of that areal index, and one of the rows flags all of its 8 bricks of that areal index.
All inputs are finite; a program needn't handle non-finite values.
Results may differ from the reference program's by a relative error of at most 0.0003.
Values sent between devices are 32-bit elements; how exact they have to be, the bound alone decides.
A program may use at most 128 MiB of HBM per device.

```python
import math
import jax
import jax.numpy as jnp
from jax import lax

NCOMP = 9
NZ = 8
BX = 4
CY = 256
BRICKS = 8
SS_ITERS = 3
RR_ITERS = 3
NX = 2048
NY = 1024
XBRICKS = 512
N_LAYER = 4


def draw_two_phase(key, part):
    groups = XBRICKS // BRICKS
    spare_units = (N_LAYER - 2) * (BRICKS // 2)
    key_heavy = jax.random.fold_in(key, 11)
    key_units = jax.random.fold_in(key, 23)
    key_scores = jax.random.fold_in(key, 37)
    heavy_device = jax.random.randint(key_heavy, (groups,), 0, N_LAYER)
    picked_units = jax.random.randint(key_units, (groups, spare_units), 0, N_LAYER - 1)
    target = (heavy_device[:, None] + 1 + picked_units) % N_LAYER
    counts = jnp.sum((target[:, :, None] == jnp.arange(N_LAYER)[None, None, :]).astype(jnp.int32), axis=1)
    counts = jnp.where(jnp.arange(N_LAYER)[None, :] == heavy_device[:, None], BRICKS, counts)
    scores = jax.random.randint(key_scores, (groups, N_LAYER, BRICKS), 0, 1 << 20) * BRICKS + jnp.arange(BRICKS)[None, None, :]
    ranking = jnp.argsort(jnp.argsort(scores, axis=-1), axis=-1)
    flagged = (ranking < counts[:, :, None]).astype(jnp.int32)
    return jnp.transpose(flagged, (1, 0, 2)).reshape(N_LAYER, groups * BRICKS)


def steps_of(key, shape, shards, low, largest):
    factor_of, own = 1.0, jax.random.fold_in(key, 6)
    for position, shards_of in shards:
        heights = jnp.exp(jax.random.uniform(jax.random.fold_in(own, position), (shards_of,), jnp.float32, low / len(shards), largest / len(shards)))
        factor_of = factor_of * jnp.repeat(heights, shape[position] // shards_of).reshape([-1 if axis == position else 1 for axis in range(len(shape))])
    return factor_of


def normal_values(rng, extent, deviation, most, held_as=jnp.bfloat16):
    entries = jax.random.normal(rng, extent, jnp.float32) * deviation
    return jnp.minimum(jnp.maximum(entries, -most), most).astype(held_as)


def setup_inputs(seed: int = 0) -> dict:
    key_list = jax.random.split(jax.random.key(seed), 12)
    return {
        "pressure": jnp.clip(0.7 + 0.7 * jax.random.uniform(key_list[0], (NZ, NX, NY), jnp.float32) ** steps_of(key_list[0], (NZ, NX, NY), ((1, 64), (2, 4)), -0.2, 0.2), 0.7, 1.4),
        "composition": jnp.clip(jnp.exp(math.log(1.0) - 3.912023 * jax.random.uniform(key_list[1], (NCOMP, NZ, NX, NY), jnp.float32) ** steps_of(key_list[1], (NCOMP, NZ, NX, NY), ((2, 64), (3, 4)), -0.2, 0.2)), 0.02, 1.0),
        "mass_old": jnp.clip(0.3 * jax.random.uniform(key_list[2], (NCOMP, NZ, NX, NY), jnp.float32) ** steps_of(key_list[2], (NCOMP, NZ, NX, NY), ((2, 64), (3, 4)), -0.2, 0.2), 0.0, 0.3),
        "pore_volume": jnp.clip(jnp.exp(math.log(2.0) - 1.3862944 * jax.random.uniform(key_list[3], (NZ, NX, NY), jnp.float32) ** steps_of(key_list[3], (NZ, NX, NY), ((1, 64), (2, 4)), -0.2, 0.2)), 0.5, 2.0),
        "trans_x": jnp.clip(jnp.exp(math.log(3.0) - 2.3025851 * jax.random.uniform(key_list[4], (NZ, NX, NY), jnp.float32) ** steps_of(key_list[4], (NZ, NX, NY), ((1, 64), (2, 4)), -0.2, 0.2)), 0.3, 3.0),
        "trans_y": jnp.clip(jnp.exp(math.log(3.0) - 2.3025851 * jax.random.uniform(key_list[5], (NZ, NX, NY), jnp.float32) ** steps_of(key_list[5], (NZ, NX, NY), ((1, 64), (2, 4)), -0.2, 0.2)), 0.3, 3.0),
        "trans_z": jnp.clip(jnp.exp(math.log(3.0) - 2.3025851 * jax.random.uniform(key_list[6], (NZ, NX, NY), jnp.float32) ** steps_of(key_list[6], (NZ, NX, NY), ((1, 64), (2, 4)), -0.2, 0.2)), 0.3, 3.0),
        "volatility": jnp.clip(jax.random.uniform(key_list[7], (NCOMP,), jnp.float32, 1.5, 3.0), 1.5, 3.0),
        "pressure_slope": jnp.clip(jax.random.uniform(key_list[8], (NCOMP,), jnp.float32, 0.2, 1.0), 0.2, 1.0),
        "mixing": normal_values(key_list[9], (NCOMP, NCOMP), 3 ** -0.5, 3.5, jnp.float32),
        "two_phase": draw_two_phase(jax.random.fold_in(key_list[11], 71), 0),
    }


light_count = 4
liquid_visc = 1.0
vapour_visc = 0.25
time_step = 4.0
compress = 0.2


def flash(pressure, feed, volatility, pressure_slope, mixing):
    expand = (-1,) + (1,) * pressure.ndim
    component_sign = jnp.where(jnp.arange(feed.shape[0]) < light_count, 1.0, -1.0).astype(jnp.float32)
    base_log = (component_sign * volatility).reshape(expand) - pressure_slope.reshape(expand) * jnp.log(pressure)[None]
    liquid = feed
    vapour = feed
    fraction = jnp.zeros(pressure.shape, jnp.float32)
    for outer_step in range(SS_ITERS):
        log_ratio = base_log + jnp.tanh(jnp.tensordot(mixing, liquid - vapour, axes=1, precision=lax.Precision.HIGHEST))
        k_value = jnp.exp(log_ratio)
        excess = k_value - 1.0
        fraction = jnp.full(pressure.shape, 0.5, jnp.float32)
        for inner_step in range(RR_ITERS):
            scaled = excess / (1.0 + fraction[None] * excess)
            mismatch = jnp.sum(feed * scaled, axis=0)
            gradient = jnp.sum(feed * scaled * scaled, axis=0)
            fraction = jnp.clip(fraction + mismatch / gradient, 0.0, 1.0)
        liquid = feed / (1.0 + fraction[None] * excess)
        vapour = k_value * liquid
    return ((1.0 - fraction) ** 2 / liquid_visc) * liquid + (fraction ** 2 / vapour_visc) * vapour


def neighbours(field):
    centre = field[..., 1:-1, 1:-1, 1:-1]
    beside = [field[..., 2:, 1:-1, 1:-1], field[..., :-2, 1:-1, 1:-1],
              field[..., 1:-1, 2:, 1:-1], field[..., 1:-1, :-2, 1:-1],
              field[..., 1:-1, 1:-1, 2:], field[..., 1:-1, 1:-1, :-2]]
    return centre, beside


def assemble(pressure, mobility, trans_z, trans_x, trans_y):
    press_here, press_near = neighbours(pressure)
    mobility_here, mobility_near = neighbours(mobility)
    total_here = jnp.sum(mobility_here, axis=0)
    depth_faces = neighbours(trans_z)
    first_faces = neighbours(trans_x)
    second_faces = neighbours(trans_y)
    faces = [depth_faces[0], depth_faces[1][1], first_faces[0], first_faces[1][3], second_faces[0], second_faces[1][5]]
    flux = jnp.zeros(mobility_here.shape, jnp.float32)
    couplings = []
    for face_index in range(6):
        strength = time_step * faces[face_index]
        flux = flux + strength * (press_here - press_near[face_index]) * (0.5 * (mobility_here + mobility_near[face_index]))
        couplings.append(strength * (0.5 * (total_here + jnp.sum(mobility_near[face_index], axis=0))))
    return flux, couplings


def reference(pressure, composition, mass_old, pore_volume, trans_x, trans_y, trans_z, volatility, pressure_slope, mixing, two_phase):
    feed_norm = composition / jnp.sum(composition, axis=0, keepdims=True)

    def flash_level(pieces):
        return flash(pieces[0], pieces[1], volatility, pressure_slope, mixing)

    two_mobility = lax.map(flash_level, (pressure, jnp.moveaxis(feed_norm, 1, 0)))
    two_mobility = jnp.moveaxis(two_mobility, 0, 1)
    cell_flags = jnp.transpose(jnp.repeat(jnp.repeat(two_phase, CY, axis=0), BX, axis=1))
    mobility = jnp.where(cell_flags[None, None, :, :] > 0, two_mobility, feed_norm / liquid_visc)
    keep_x = jnp.where(jnp.arange(NX)[None, :, None] < NX - 1, trans_x, 0.0)
    keep_y = jnp.where(jnp.arange(NY)[None, None, :] < NY - 1, trans_y, 0.0)
    keep_z = jnp.where(jnp.arange(NZ)[:, None, None] < NZ - 1, trans_z, 0.0)
    flux, couplings = assemble(jnp.pad(pressure, 1), jnp.pad(mobility, ((0, 0), (1, 1), (1, 1), (1, 1))),
                               jnp.pad(keep_z, 1), jnp.pad(keep_x, 1), jnp.pad(keep_y, 1))
    residual = pore_volume * feed_norm - mass_old + flux
    total = jnp.sum(residual, axis=0)
    diagonal = pore_volume * compress
    for face_index in range(6):
        diagonal = diagonal + couplings[face_index]
    first = -total / diagonal
    near = neighbours(jnp.pad(first, 1))[1]
    gathered = -total
    for face_index in range(6):
        gathered = gathered + couplings[face_index] * near[face_index]
    second = gathered / diagonal
    return residual, pressure + second
```

```python
import functools

import jax
import jax.numpy as jnp
from jax import lax
from jax.experimental import pallas as pl
from jax.experimental.pallas import tpu as pltpu
from jax.sharding import PartitionSpec as P

SS_ITERS = 3
RR_ITERS = 3
light_count = 4
compress = 0.2
F32 = jnp.float32
BF16 = jnp.bfloat16
MESH = pl.DeviceIdType.MESH
TILE = 8
FIELDS = 12
YROWS = 16
VMEM_BYTES = 24 << 20


def total_of(values):
    return functools.reduce(lambda a, b: a + b, values)


def split_matrix(mix, comps):
    size = comps * TILE
    rows = lax.broadcasted_iota(jnp.int32, (size, comps), 0) // TILE
    cols = lax.broadcasted_iota(jnp.int32, (size, comps), 1)
    pick = (rows == cols).astype(F32)
    wide = lax.dot_general(
        jnp.dot(pick, mix, precision=lax.Precision.HIGHEST, preferred_element_type=F32),
        pick,
        (((1,), (1,)), ((), ())),
        precision=lax.Precision.HIGHEST,
        preferred_element_type=F32,
    )
    a = lax.broadcasted_iota(jnp.int32, (size, size), 0) % TILE
    b = lax.broadcasted_iota(jnp.int32, (size, size), 1) % TILE
    full = jnp.where(a == b, 2.0 * wide, 0.0)
    high = full.astype(BF16)
    return high, (full - high.astype(F32)).astype(BF16)


def mixed(w_ref, parts):
    stack = jnp.concatenate(parts, axis=0)
    high = stack.astype(BF16)
    low = (stack - high.astype(F32)).astype(BF16)
    out = (
        jnp.dot(w_ref[0], high, preferred_element_type=F32)
        + jnp.dot(w_ref[1], high, preferred_element_type=F32)
        + jnp.dot(w_ref[0], low, preferred_element_type=F32)
    )
    return [out[i * TILE : (i + 1) * TILE] for i in range(len(parts))]


def flash(feed, log_p, half_vol, half_slope, w_ref):
    comps = len(feed)
    base = [half_vol[i] - half_slope[i] * log_p for i in range(comps)]
    half_log = base
    moved = None
    for outer in range(SS_ITERS):
        if outer:
            pulled = mixed(w_ref, moved)
            half_log = [base[i] - 0.5 * jnp.tanh(pulled[i]) for i in range(comps)]
        q = [jnp.tanh(v) for v in half_log]
        h = [1.0 / v for v in q]
        centre = None
        for inner in range(RR_ITERS):
            if inner:
                q = [1.0 / (h[i] + centre) for i in range(comps)]
            fq = [feed[i] * q[i] for i in range(comps)]
            step = total_of(fq) / total_of([fq[i] * q[i] for i in range(comps)])
            centre = jnp.clip(step if centre is None else centre + step, -1.0, 1.0)
        moved = [feed[i] * (1.0 / (h[i] + centre)) for i in range(comps)]
    low = 1.0 - centre
    high = 1.0 + centre
    low = 0.25 * (low * low)
    high = high * high
    outer_sum, outer_diff = low + high, high - low
    return [moved[i] * (outer_sum * h[i] + outer_diff) for i in range(comps)]


def flash_kernel(
    comps,
    p_hbm, comp_hbm, mass_hbm, pv_hbm, tx_hbm, ty_hbm, tz_hbm, vol_hbm, slope_hbm, mix_hbm, two_hbm,
    comp, mass, mob, pvi, grads, xmob, ymob, newp,
    p, pv, tx, ty, tz, w_ref, mix, vol, slope, two, flags,
    msum, fsum, first, rest, rdiag, coup, mxh, myh,
    xsend, xrecv, ysend, yrecv, fxsend, fxrecv, fysend, fyrecv,
    in_sem, send_sem, recv_sem, send2_sem, recv2_sem,
):
    depth, width, span = p.shape
    here_a = lax.axis_index("areal")
    here_l = lax.axis_index("layer")
    na = lax.axis_size("areal")
    nl = lax.axis_size("layer")
    xm = (lax.rem(here_a + na - 1, na), here_l)
    xp = (lax.rem(here_a + 1, na), here_l)
    ym = (here_a, lax.rem(here_l + nl - 1, nl))
    yp = (here_a, lax.rem(here_l + 1, nl))

    loads = [
        pltpu.make_async_copy(src, dst, in_sem.at[i])
        for i, (src, dst) in enumerate(
            [
                (mix_hbm, mix), (vol_hbm, vol), (slope_hbm, slope), (two_hbm, two),
                (comp_hbm, comp), (p_hbm, p), (tx_hbm, tx), (ty_hbm, ty),
                (mass_hbm, mass), (pv_hbm, pv), (tz_hbm, tz),
            ]
        )
    ]
    for load in loads:
        load.start()
    barrier = pltpu.get_barrier_semaphore()
    for device in (xm, xp, ym, yp):
        pl.semaphore_signal(barrier, inc=1, device_id=device, device_id_type=MESH)
    for load in loads[:4]:
        load.wait()
    w_ref[0], w_ref[1] = split_matrix(mix[...], comps)
    half_vol = [(0.5 if i < light_count else -0.5) * vol[i] for i in range(comps)]
    half_slope = [0.5 * slope[i] for i in range(comps)]
    bricks = two.shape[1]
    brick_of = lax.broadcasted_iota(jnp.int32, (width, span), 0) // (width // bricks)
    flag = jnp.zeros((width, span), F32)
    for b in range(bricks):
        flag = jnp.where(brick_of == b, two[here_l, b].astype(F32), flag)
    flags[...] = flag
    for load in loads[4:8]:
        load.wait()

    lane = lax.broadcasted_iota(jnp.int32, (width, 128), 1)

    def pack(z, carry):
        packed = jnp.zeros((width, 128), F32)
        for side, cut in ((0, 0), (1, span - 128)):
            source = 0 if side == 0 else 127
            for k in range(FIELDS):
                if k < comps:
                    value = comp[k, z, :, cut : cut + 128]
                elif k == comps:
                    value = p[z, :, cut : cut + 128]
                elif k == comps + 1:
                    value = ty[z, :, cut : cut + 128]
                else:
                    value = flags[:, cut : cut + 128]
                target = side * YROWS + k
                moved = pltpu.roll(value, (target - source) % 128, 1)
                packed = jnp.where(lane == target, moved, packed)
        ymob[pl.ds(pl.multiple_of(z * width, width), width), :] = packed
        for side, row in ((0, 0), (1, width - 1)):
            for k in range(comps):
                xsend[side, k, pl.ds(z, 1), :] = comp[k, z, row : row + 1, :]
            xsend[side, comps, pl.ds(z, 1), :] = p[z, row : row + 1, :]
            xsend[side, comps + 1, pl.ds(z, 1), :] = tx[z, row : row + 1, :]
            xsend[side, comps + 2, pl.ds(z, 1), :] = flags[row : row + 1, :]
        return carry

    lax.fori_loop(0, depth, pack, 0)
    turned = jnp.transpose(ymob[...])
    ysend[0] = turned[:YROWS]
    ysend[1] = turned[YROWS : 2 * YROWS]
    pl.semaphore_wait(barrier, 4)
    sends = [
        pltpu.make_async_remote_copy(
            src_ref=src, dst_ref=dst, send_sem=send_sem.at[i], recv_sem=recv_sem.at[i],
            device_id=device, device_id_type=MESH,
        )
        for i, (src, dst, device) in enumerate(
            [
                (xsend.at[0], xrecv.at[1], xm), (xsend.at[1], xrecv.at[0], xp),
                (ysend.at[0], yrecv.at[1], ym), (ysend.at[1], yrecv.at[0], yp),
            ]
        )
    ]
    for send in sends:
        send.start()

    def cells(values, pressure, flagged):
        total = total_of(values)
        inverse = 1.0 / total
        feed = [v * inverse for v in values]
        moved = flash(feed, jnp.log(pressure), half_vol, half_slope, w_ref)
        return inverse, total * inverse, [
            jnp.where(flagged > 0.0, moved[i], feed[i]) for i in range(comps)
        ]

    blocks = width // TILE

    def block(step, carry):
        z = step // blocks
        rows = pl.ds(pl.multiple_of((step % blocks) * TILE, TILE), TILE)
        values = [comp[i, z, rows, :] for i in range(comps)]
        inverse, whole, found = cells(values, p[z, rows, :], flags[rows, :])
        pvi[z, rows, :] = inverse
        fsum[z, rows, :] = whole
        for i in range(comps):
            mob[i, z, rows, :] = found[i]
        msum[z, rows, :] = total_of(found)
        return carry

    lax.fori_loop(0, depth * blocks, block, 0, unroll=8)

    for load in loads[8:]:
        load.wait()
    for send in sends:
        send.wait()

    for side in range(2):
        values = [xrecv[side, k] for k in range(comps)]
        _, _, found = cells(values, xrecv[side, comps], xrecv[side, comps + 2])
        for i in range(comps):
            xmob[side, i] = found[i]
        mxh[side] = total_of(found)
    sub = lax.broadcasted_iota(jnp.int32, (TILE, span), 0)

    def both(k):
        return jnp.where(sub == 0, yrecv[0, k : k + 1, :], yrecv[1, k : k + 1, :])

    _, _, found = cells([both(k) for k in range(comps)], both(comps), both(comps + 2))
    together = found + [total_of(found), both(comps), both(comps + 1)]
    for side in range(2):
        for k, value in enumerate(together):
            myh[side * YROWS + k : side * YROWS + k + 1, :] = value[side : side + 1, :]
    ymob[...] = jnp.transpose(myh[...])

    row_id = lax.broadcasted_iota(jnp.int32, (width, span), 0)
    lane_id = lax.broadcasted_iota(jnp.int32, (width, span), 1)
    has_xm = (here_a > 0).astype(F32)
    has_xp = (here_a < na - 1).astype(F32)
    has_ym = (here_l > 0).astype(F32)
    has_yp = (here_l < nl - 1).astype(F32)

    def before_x(value, edge):
        return jnp.where(row_id == 0, edge, pltpu.roll(value, 1, 0))

    def after_x(value, edge):
        return jnp.where(row_id == width - 1, edge, pltpu.roll(value, width - 1, 0))

    def before_y(value, edge):
        return jnp.where(lane_id == 0, edge, pltpu.roll(value, 1, 1))

    def after_y(value, edge):
        return jnp.where(lane_id == span - 1, edge, pltpu.roll(value, span - 1, 1))

    def faces(z, carry):
        up = jnp.minimum(z + 1, depth - 1)
        down = jnp.maximum(z - 1, 0)
        zrow = pl.ds(z, 1)
        yrow = pl.ds(pl.multiple_of(z * width, width), width)
        here_p, here_m = p[z], msum[z]
        edge = ymob[yrow, :]
        em = [edge[:, k : k + 1] for k in (comps, comps + 1, comps + 2)]
        ep = [edge[:, YROWS + k : YROWS + k + 1] for k in (comps, comps + 1)]
        t_x, t_y = tx[z], ty[z]
        strength = [
            tz[z] * (z < depth - 1).astype(F32),
            tz[down] * (z > 0).astype(F32),
            jnp.where(row_id == width - 1, has_xp * t_x, t_x),
            before_x(t_x, has_xm * xrecv[0, comps + 1, zrow, :]),
            jnp.where(lane_id == span - 1, has_yp * t_y, t_y),
            before_y(t_y, has_ym * em[2]),
        ]
        near_p = [
            p[up], p[down],
            after_x(here_p, xrecv[1, comps, zrow, :]), before_x(here_p, xrecv[0, comps, zrow, :]),
            after_y(here_p, ep[1]), before_y(here_p, em[1]),
        ]
        near_m = [
            msum[up], msum[down],
            after_x(here_m, mxh[1, zrow, :]), before_x(here_m, mxh[0, zrow, :]),
            after_y(here_m, ep[0]), before_y(here_m, em[0]),
        ]
        volume = pv[z]
        balance = volume * fsum[z] - total_of([mass[i, z] for i in range(comps)])
        diagonal = compress * volume
        centre = None
        for f in range(6):
            twice = 2.0 * strength[f]
            fall = here_p - near_p[f]
            link = twice * (here_m + near_m[f])
            slope_f = twice * fall
            balance = balance + link * fall
            diagonal = diagonal + link
            grads[f, z] = slope_f
            coup[f, z] = link
            centre = slope_f if centre is None else centre + slope_f
        grads[6, z] = centre
        inverse = 1.0 / diagonal
        update = -balance * inverse
        first[z] = update
        rest[z] = -balance
        rdiag[z] = inverse
        pvi[z] = volume * pvi[z]
        fxsend[0, zrow, :] = update[0:1, :]
        fxsend[1, zrow, :] = update[width - 1 : width, :]
        left = update[:, 0:128]
        right = pltpu.roll(update[:, span - 128 : span], 2, 1)
        coup[6, z, :, 0:128] = jnp.where(lane == 0, left, right)
        return carry

    lax.fori_loop(0, depth, faces, 0)
    stacked = coup[6, :, :, 0:128].reshape(depth * width, 128)
    fysend[...] = jnp.transpose(stacked)[:TILE]
    sends = [
        pltpu.make_async_remote_copy(
            src_ref=src, dst_ref=dst, send_sem=send2_sem.at[i], recv_sem=recv2_sem.at[i],
            device_id=device, device_id_type=MESH,
        )
        for i, (src, dst, device) in enumerate(
            [
                (fxsend.at[0], fxrecv.at[1], xm), (fxsend.at[1], fxrecv.at[0], xp),
                (fysend, fyrecv.at[1], ym), (fysend, fyrecv.at[0], yp),
            ]
        )
    ]
    for send in sends:
        send.start()
    for send in sends:
        send.wait()
    myh[0:1, :] = fyrecv[0, 1:2, :]
    myh[1:2, :] = fyrecv[1, 0:1, :]
    coup[6, :, :, 0:128] = jnp.transpose(myh[...]).reshape(depth, width, 128)

    def update(z, carry):
        up = jnp.minimum(z + 1, depth - 1)
        down = jnp.maximum(z - 1, 0)
        zrow = pl.ds(z, 1)
        value = first[z]
        edge = coup[6, z, :, 0:128]
        near = [
            first[up], first[down],
            after_x(value, fxrecv[1, zrow, :]), before_x(value, fxrecv[0, zrow, :]),
            after_y(value, edge[:, 1:2]), before_y(value, edge[:, 0:1]),
        ]
        gathered = rest[z]
        for f in range(6):
            gathered = gathered + coup[f, z] * near[f]
        newp[z] = p[z] + gathered * rdiag[z]
        return carry

    lax.fori_loop(0, depth, update, 0)


def residual_kernel(
    comps, comp, mass, mob, pvi, grads, xmob, ymob, newp, out_hbm, newp_hbm, out, sem
):
    depth, width, span = pvi.shape
    row_id = lax.broadcasted_iota(jnp.int32, (width, span), 0)
    lane_id = lax.broadcasted_iota(jnp.int32, (width, span), 1)

    def level(z, i):
        up = jnp.minimum(z + 1, depth - 1)
        down = jnp.maximum(z - 1, 0)
        zrow = pl.ds(z, 1)
        here = mob[i, z]
        edge = ymob[pl.ds(pl.multiple_of(z * width, width), width), :]
        near = [
            mob[i, up],
            mob[i, down],
            jnp.where(row_id == width - 1, xmob[1, i, zrow, :], pltpu.roll(here, width - 1, 0)),
            jnp.where(row_id == 0, xmob[0, i, zrow, :], pltpu.roll(here, 1, 0)),
            jnp.where(
                lane_id == span - 1,
                edge[:, YROWS + i : YROWS + i + 1],
                pltpu.roll(here, span - 1, 1),
            ),
            jnp.where(lane_id == 0, edge[:, i : i + 1], pltpu.roll(here, 1, 1)),
        ]
        value = pvi[z] * comp[i, z] - mass[i, z] + grads[6, z] * here
        for f in range(6):
            value = value + grads[f, z] * near[f]
        out[i, z] = value

    copies = [pltpu.make_async_copy(newp, newp_hbm, sem.at[comps])]
    copies[0].start()
    for i in range(comps):

        def body(z, carry, i=i):
            level(z, i)
            return carry

        lax.fori_loop(0, depth, body, 0)
        copy = pltpu.make_async_copy(out.at[i], out_hbm.at[i], sem.at[i])
        copy.start()
        copies.append(copy)
    for copy in copies:
        copy.wait()


def on_device(
    pressure, composition, mass_old, pore_volume, trans_x, trans_y, trans_z,
    volatility, pressure_slope, mixing, two_phase,
):
    comps = composition.shape[0]
    grid = pressure.shape
    depth, width, span = grid
    big = (comps,) + grid
    anywhere = pl.BlockSpec(memory_space=pltpu.HBM)
    local = pl.BlockSpec(memory_space=pltpu.VMEM)
    dma = pltpu.SemaphoreType.DMA

    def array(shape):
        return jax.ShapeDtypeStruct(shape, F32)

    def scratch(shape):
        return pltpu.VMEM(shape, F32)

    comp, mass, mob, pvi, grads, xmob, ymob, newp = pl.pallas_call(
        functools.partial(flash_kernel, comps),
        name="flash",
        out_shape=(
            array(big), array(big), array(big), array(grid), array((7,) + grid),
            array((2, comps, depth, span)), array((depth * width, 128)), array(grid),
        ),
        in_specs=[anywhere] * 11,
        out_specs=(local,) * 8,
        scratch_shapes=[
            scratch(grid), scratch(grid), scratch(grid), scratch(grid), scratch(grid),
            pltpu.VMEM((2, comps * TILE, comps * TILE), BF16),
            scratch((comps, comps)),
            pltpu.SMEM((comps,), F32), pltpu.SMEM((comps,), F32),
            pltpu.SMEM(two_phase.shape, jnp.int32),
            scratch((width, span)),
            scratch(grid), scratch(grid), scratch(grid), scratch(grid), scratch(grid),
            scratch((7,) + grid),
            scratch((2, depth, span)), scratch((128, depth * width)),
            scratch((2, FIELDS, depth, span)), scratch((2, FIELDS, depth, span)),
            scratch((2, YROWS, depth * width)), scratch((2, YROWS, depth * width)),
            scratch((2, depth, span)), scratch((2, depth, span)),
            scratch((TILE, depth * width)), scratch((2, TILE, depth * width)),
            dma((11,)), dma((4,)), dma((4,)), dma((4,)), dma((4,)),
        ],
        compiler_params=pltpu.CompilerParams(
            collective_id=0, has_side_effects=True, vmem_limit_bytes=VMEM_BYTES
        ),
    )(
        *(
            pltpu.with_memory_space_constraint(value, pltpu.HBM)
            for value in (
                pressure, composition, mass_old, pore_volume, trans_x, trans_y, trans_z,
                volatility, pressure_slope, mixing, two_phase,
            )
        )
    )
    return pl.pallas_call(
        functools.partial(residual_kernel, comps),
        name="residual",
        out_shape=(array(big), array(grid)),
        in_specs=[local] * 8,
        out_specs=(anywhere, anywhere),
        scratch_shapes=[scratch(big), dma((comps + 1,))],
        compiler_params=pltpu.CompilerParams(vmem_limit_bytes=VMEM_BYTES),
    )(comp, mass, mob, pvi, grads, xmob, ymob, newp)


def solution(mesh):
    placed = (
        P(None, "areal", "layer"),
        P(None, None, "areal", "layer"),
        P(None, None, "areal", "layer"),
        P(None, "areal", "layer"),
        P(None, "areal", "layer"),
        P(None, "areal", "layer"),
        P(None, "areal", "layer"),
        P(),
        P(),
        P(),
        P(None, "areal"),
    )
    return jax.shard_map(
        on_device,
        mesh=mesh,
        in_specs=placed,
        out_specs=(P(None, None, "areal", "layer"), P(None, "areal", "layer")),
        check_vma=False,
    )
```

```python
import functools

import jax
import jax.numpy as jnp
from jax import lax
from jax.experimental import pallas as pl
from jax.experimental.pallas import tpu as pltpu
from jax.sharding import PartitionSpec as P

SS_ITERS = 3
RR_ITERS = 3
light_count = 4
compress = 0.2
F32 = jnp.float32
BF16 = jnp.bfloat16
MESH = pl.DeviceIdType.MESH
TILE = 8
FIELDS = 12
YROWS = 16
VMEM_BYTES = 24 << 20


def total_of(values):
    return functools.reduce(lambda a, b: a + b, values)


def split_matrix(mix, comps):
    size = comps * TILE
    rows = lax.broadcasted_iota(jnp.int32, (size, comps), 0) // TILE
    cols = lax.broadcasted_iota(jnp.int32, (size, comps), 1)
    pick = (rows == cols).astype(F32)
    wide = lax.dot_general(
        jnp.dot(pick, mix, precision=lax.Precision.HIGHEST, preferred_element_type=F32),
        pick,
        (((1,), (1,)), ((), ())),
        precision=lax.Precision.HIGHEST,
        preferred_element_type=F32,
    )
    a = lax.broadcasted_iota(jnp.int32, (size, size), 0) % TILE
    b = lax.broadcasted_iota(jnp.int32, (size, size), 1) % TILE
    full = jnp.where(a == b, 2.0 * wide, 0.0)
    high = full.astype(BF16)
    return high, (full - high.astype(F32)).astype(BF16)


def mixed(w_ref, parts):
    stack = jnp.concatenate(parts, axis=0)
    high = stack.astype(BF16)
    low = (stack - high.astype(F32)).astype(BF16)
    out = (
        jnp.dot(w_ref[0], high, preferred_element_type=F32)
        + jnp.dot(w_ref[1], high, preferred_element_type=F32)
        + jnp.dot(w_ref[0], low, preferred_element_type=F32)
    )
    return [out[i * TILE : (i + 1) * TILE] for i in range(len(parts))]


def flash(feed, log_p, half_vol, half_slope, w_ref):
    comps = len(feed)
    base = [half_vol[i] - half_slope[i] * log_p for i in range(comps)]
    half_log = base
    moved = None
    for outer in range(SS_ITERS):
        if outer:
            pulled = mixed(w_ref, moved)
            half_log = [base[i] - 0.5 * jnp.tanh(pulled[i]) for i in range(comps)]
        q = [jnp.tanh(v) for v in half_log]
        h = [1.0 / v for v in q]
        centre = None
        for inner in range(RR_ITERS):
            if inner:
                q = [1.0 / (h[i] + centre) for i in range(comps)]
            fq = [feed[i] * q[i] for i in range(comps)]
            step = total_of(fq) / total_of([fq[i] * q[i] for i in range(comps)])
            centre = jnp.clip(step if centre is None else centre + step, -1.0, 1.0)
        moved = [feed[i] * (1.0 / (h[i] + centre)) for i in range(comps)]
    low = 1.0 - centre
    high = 1.0 + centre
    low = 0.25 * (low * low)
    high = high * high
    outer_sum, outer_diff = low + high, high - low
    return [moved[i] * (outer_sum * h[i] + outer_diff) for i in range(comps)]


def flash_kernel(
    comps,
    p_hbm, comp_hbm, mass_hbm, pv_hbm, tx_hbm, ty_hbm, tz_hbm, vol_hbm, slope_hbm, mix_hbm, two_hbm,
    out, newp,
    comp, mass, mob, pvi, grads, xmob, ymob, p, pv, tx, ty, tz, w_ref, mix, vol, slope, two, flags,
    msum, fsum, first, rest, rdiag, coup, mxh, myh,
    xsend, xrecv, ysend, yrecv, fxsend, fxrecv, fysend, fyrecv,
    in_sem, send_sem, recv_sem, send2_sem, recv2_sem,
):
    depth, width, span = p.shape
    here_a = lax.axis_index("areal")
    here_l = lax.axis_index("layer")
    na = lax.axis_size("areal")
    nl = lax.axis_size("layer")
    xm = (lax.rem(here_a + na - 1, na), here_l)
    xp = (lax.rem(here_a + 1, na), here_l)
    ym = (here_a, lax.rem(here_l + nl - 1, nl))
    yp = (here_a, lax.rem(here_l + 1, nl))

    loads = [
        pltpu.make_async_copy(src, dst, in_sem.at[i])
        for i, (src, dst) in enumerate(
            [
                (mix_hbm, mix), (vol_hbm, vol), (slope_hbm, slope), (two_hbm, two),
                (comp_hbm, comp), (p_hbm, p), (tx_hbm, tx), (ty_hbm, ty),
                (mass_hbm, mass), (pv_hbm, pv), (tz_hbm, tz),
            ]
        )
    ]
    for load in loads:
        load.start()
    barrier = pltpu.get_barrier_semaphore()
    there = (here_a > 0, here_a < na - 1, here_l > 0, here_l < nl - 1)

    def finish(sends):
        when_there(send.wait_send for send in sends)
        when_there(sends[i].wait_recv for i in (1, 0, 3, 2))

    def when_there(actions):
        for exists, action in zip(there, actions):
            pl.when(exists)(action)

    when_there(
        functools.partial(
            pl.semaphore_signal, barrier, inc=1, device_id=device, device_id_type=MESH
        )
        for device in (xm, xp, ym, yp)
    )
    for load in loads[:4]:
        load.wait()
    w_ref[0], w_ref[1] = split_matrix(mix[...], comps)
    half_vol = [(0.5 if i < light_count else -0.5) * vol[i] for i in range(comps)]
    half_slope = [0.5 * slope[i] for i in range(comps)]
    bricks = two.shape[1]
    brick_of = lax.broadcasted_iota(jnp.int32, (width, span), 0) // (width // bricks)
    flag = jnp.zeros((width, span), F32)
    for b in range(bricks):
        flag = jnp.where(brick_of == b, two[here_l, b].astype(F32), flag)
    flags[...] = flag
    for load in loads[4:8]:
        load.wait()

    lane = lax.broadcasted_iota(jnp.int32, (width, 128), 1)

    def pack(z, carry):
        packed = jnp.zeros((width, 128), F32)
        for side, cut in ((0, 0), (1, span - 128)):
            source = 0 if side == 0 else 127
            for k in range(FIELDS):
                if k < comps:
                    value = comp[k, z, :, cut : cut + 128]
                elif k == comps:
                    value = p[z, :, cut : cut + 128]
                elif k == comps + 1:
                    value = ty[z, :, cut : cut + 128]
                else:
                    value = flags[:, cut : cut + 128]
                target = side * YROWS + k
                moved = pltpu.roll(value, (target - source) % 128, 1)
                packed = jnp.where(lane == target, moved, packed)
        ymob[pl.ds(pl.multiple_of(z * width, width), width), :] = packed
        for side, row in ((0, 0), (1, width - 1)):
            for k in range(comps):
                xsend[side, k, pl.ds(z, 1), :] = comp[k, z, row : row + 1, :]
            xsend[side, comps, pl.ds(z, 1), :] = p[z, row : row + 1, :]
            xsend[side, comps + 1, pl.ds(z, 1), :] = tx[z, row : row + 1, :]
            xsend[side, comps + 2, pl.ds(z, 1), :] = flags[row : row + 1, :]
        return carry

    lax.fori_loop(0, depth, pack, 0, unroll=4)
    turned = jnp.transpose(ymob[...])
    ysend[0] = turned[:YROWS]
    ysend[1] = turned[YROWS : 2 * YROWS]
    pl.semaphore_wait(barrier, total_of([exists.astype(jnp.int32) for exists in there]))
    sends = [
        pltpu.make_async_remote_copy(
            src_ref=src, dst_ref=dst, send_sem=send_sem.at[i], recv_sem=recv_sem.at[i],
            device_id=device, device_id_type=MESH,
        )
        for i, (src, dst, device) in enumerate(
            [
                (xsend.at[0], xrecv.at[1], xm), (xsend.at[1], xrecv.at[0], xp),
                (ysend.at[0], yrecv.at[1], ym), (ysend.at[1], yrecv.at[0], yp),
            ]
        )
    ]
    when_there(send.start for send in sends)

    for exists, slot in zip(there, (xrecv.at[0], xrecv.at[1], yrecv.at[0], yrecv.at[1])):

        @pl.when(jnp.logical_not(exists))
        def _(slot=slot):
            slot[...] = jnp.ones(slot.shape, F32)

    def cells(values, pressure, flagged):
        total = total_of(values)
        inverse = 1.0 / total
        feed = [v * inverse for v in values]
        moved = flash(feed, jnp.log(pressure), half_vol, half_slope, w_ref)
        return inverse, total * inverse, [
            jnp.where(flagged > 0.0, moved[i], feed[i]) for i in range(comps)
        ]

    blocks = width // TILE

    def block(step, carry):
        z = step // blocks
        rows = pl.ds(pl.multiple_of((step % blocks) * TILE, TILE), TILE)
        values = [comp[i, z, rows, :] for i in range(comps)]
        inverse, whole, found = cells(values, p[z, rows, :], flags[rows, :])
        pvi[z, rows, :] = inverse
        fsum[z, rows, :] = whole
        for i in range(comps):
            mob[i, z, rows, :] = found[i]
        msum[z, rows, :] = total_of(found)
        return carry

    lax.fori_loop(0, depth * blocks, block, 0, unroll=8)

    for load in loads[8:]:
        load.wait()
    finish(sends)

    for side in range(2):
        values = [xrecv[side, k] for k in range(comps)]
        _, _, found = cells(values, xrecv[side, comps], xrecv[side, comps + 2])
        for i in range(comps):
            xmob[side, i] = found[i]
        mxh[side] = total_of(found)
    sub = lax.broadcasted_iota(jnp.int32, (TILE, span), 0)

    def both(k):
        return jnp.where(sub == 0, yrecv[0, k : k + 1, :], yrecv[1, k : k + 1, :])

    _, _, found = cells([both(k) for k in range(comps)], both(comps), both(comps + 2))
    together = found + [total_of(found), both(comps), both(comps + 1)]
    for side in range(2):
        for k, value in enumerate(together):
            myh[side * YROWS + k : side * YROWS + k + 1, :] = value[side : side + 1, :]
    ymob[...] = jnp.transpose(myh[...])

    row_id = lax.broadcasted_iota(jnp.int32, (width, span), 0)
    lane_id = lax.broadcasted_iota(jnp.int32, (width, span), 1)
    has_xm = (here_a > 0).astype(F32)
    has_xp = (here_a < na - 1).astype(F32)
    has_ym = (here_l > 0).astype(F32)
    has_yp = (here_l < nl - 1).astype(F32)

    def before_x(value, edge):
        return jnp.where(row_id == 0, edge, pltpu.roll(value, 1, 0))

    def after_x(value, edge):
        return jnp.where(row_id == width - 1, edge, pltpu.roll(value, width - 1, 0))

    def before_y(value, edge):
        return jnp.where(lane_id == 0, edge, pltpu.roll(value, 1, 1))

    def after_y(value, edge):
        return jnp.where(lane_id == span - 1, edge, pltpu.roll(value, span - 1, 1))

    def faces(z, carry):
        up = jnp.minimum(z + 1, depth - 1)
        down = jnp.maximum(z - 1, 0)
        zrow = pl.ds(z, 1)
        yrow = pl.ds(pl.multiple_of(z * width, width), width)
        here_p, here_m = p[z], msum[z]
        edge = ymob[yrow, :]
        em = [edge[:, k : k + 1] for k in (comps, comps + 1, comps + 2)]
        ep = [edge[:, YROWS + k : YROWS + k + 1] for k in (comps, comps + 1)]
        t_x, t_y = tx[z], ty[z]
        strength = [
            tz[z] * (z < depth - 1).astype(F32),
            tz[down] * (z > 0).astype(F32),
            jnp.where(row_id == width - 1, has_xp * t_x, t_x),
            before_x(t_x, has_xm * xrecv[0, comps + 1, zrow, :]),
            jnp.where(lane_id == span - 1, has_yp * t_y, t_y),
            before_y(t_y, has_ym * em[2]),
        ]
        near_p = [
            p[up], p[down],
            after_x(here_p, xrecv[1, comps, zrow, :]), before_x(here_p, xrecv[0, comps, zrow, :]),
            after_y(here_p, ep[1]), before_y(here_p, em[1]),
        ]
        near_m = [
            msum[up], msum[down],
            after_x(here_m, mxh[1, zrow, :]), before_x(here_m, mxh[0, zrow, :]),
            after_y(here_m, ep[0]), before_y(here_m, em[0]),
        ]
        volume = pv[z]
        balance = volume * fsum[z] - total_of([mass[i, z] for i in range(comps)])
        diagonal = compress * volume
        centre = None
        for f in range(6):
            twice = 2.0 * strength[f]
            fall = here_p - near_p[f]
            link = twice * (here_m + near_m[f])
            slope_f = twice * fall
            balance = balance + link * fall
            diagonal = diagonal + link
            grads[f, z] = slope_f
            coup[f, z] = link
            centre = slope_f if centre is None else centre + slope_f
        grads[6, z] = centre
        inverse = 1.0 / diagonal
        update = -balance * inverse
        first[z] = update
        rest[z] = -balance
        rdiag[z] = inverse
        pvi[z] = volume * pvi[z]
        fxsend[0, zrow, :] = update[0:1, :]
        fxsend[1, zrow, :] = update[width - 1 : width, :]
        left = update[:, 0:128]
        right = pltpu.roll(update[:, span - 128 : span], 2, 1)
        coup[6, z, :, 0:128] = jnp.where(lane == 0, left, right)
        return carry

    lax.fori_loop(0, depth, faces, 0, unroll=2)
    stacked = coup[6, :, :, 0:128].reshape(depth * width, 128)
    fysend[...] = jnp.transpose(stacked)[:TILE]
    sends = [
        pltpu.make_async_remote_copy(
            src_ref=src, dst_ref=dst, send_sem=send2_sem.at[i], recv_sem=recv2_sem.at[i],
            device_id=device, device_id_type=MESH,
        )
        for i, (src, dst, device) in enumerate(
            [
                (fxsend.at[0], fxrecv.at[1], xm), (fxsend.at[1], fxrecv.at[0], xp),
                (fysend, fyrecv.at[1], ym), (fysend, fyrecv.at[0], yp),
            ]
        )
    ]
    when_there(send.start for send in sends)

    def level(z, i):
        up = jnp.minimum(z + 1, depth - 1)
        down = jnp.maximum(z - 1, 0)
        zrow = pl.ds(z, 1)
        here = mob[i, z]
        edge = ymob[pl.ds(pl.multiple_of(z * width, width), width), :]
        near = [
            mob[i, up], mob[i, down],
            after_x(here, xmob[1, i, zrow, :]), before_x(here, xmob[0, i, zrow, :]),
            after_y(here, edge[:, YROWS + i : YROWS + i + 1]), before_y(here, edge[:, i : i + 1]),
        ]
        value = pvi[z] * comp[i, z] - mass[i, z] + grads[6, z] * here
        for f in range(6):
            value = value + grads[f, z] * near[f]
        out[i, z] = value

    for i in range(comps):

        def body(z, carry, i=i):
            level(z, i)
            return carry

        lax.fori_loop(0, depth, body, 0, unroll=8)
    finish(sends)
    for exists, slot in zip(there, (fxrecv.at[0], fxrecv.at[1], fyrecv.at[0], fyrecv.at[1])):

        @pl.when(jnp.logical_not(exists))
        def _(slot=slot):
            slot[...] = jnp.zeros(slot.shape, F32)

    myh[0:1, :] = fyrecv[0, 1:2, :]
    myh[1:2, :] = fyrecv[1, 0:1, :]
    coup[6, :, :, 0:128] = jnp.transpose(myh[...]).reshape(depth, width, 128)

    def update(z, carry):
        up = jnp.minimum(z + 1, depth - 1)
        down = jnp.maximum(z - 1, 0)
        zrow = pl.ds(z, 1)
        value = first[z]
        edge = coup[6, z, :, 0:128]
        near = [
            first[up], first[down],
            after_x(value, fxrecv[1, zrow, :]), before_x(value, fxrecv[0, zrow, :]),
            after_y(value, edge[:, 1:2]), before_y(value, edge[:, 0:1]),
        ]
        gathered = rest[z]
        for f in range(6):
            gathered = gathered + coup[f, z] * near[f]
        newp[z] = p[z] + gathered * rdiag[z]
        return carry

    lax.fori_loop(0, depth, update, 0, unroll=4)


def write_kernel(value, newp, out_hbm, newp_hbm, sem):
    copies = [
        pltpu.make_async_copy(src, dst, sem.at[i])
        for i, (src, dst) in enumerate(
            [(value, out_hbm), (newp, newp_hbm)]
        )
    ]
    for copy in copies:
        copy.start()
    for copy in copies:
        copy.wait()


def on_device(
    pressure, composition, mass_old, pore_volume, trans_x, trans_y, trans_z,
    volatility, pressure_slope, mixing, two_phase,
):
    comps = composition.shape[0]
    grid = pressure.shape
    depth, width, span = grid
    big = (comps,) + grid
    anywhere = pl.BlockSpec(memory_space=pltpu.HBM)
    local = pl.BlockSpec(memory_space=pltpu.VMEM)
    dma = pltpu.SemaphoreType.DMA

    def array(shape):
        return jax.ShapeDtypeStruct(shape, F32)

    def scratch(shape):
        return pltpu.VMEM(shape, F32)

    out, newp = pl.pallas_call(
        functools.partial(flash_kernel, comps),
        name="flash",
        out_shape=(array(big), array(grid)),
        in_specs=[anywhere] * 11,
        out_specs=(local,) * 2,
        scratch_shapes=[
            scratch(big), scratch(big), scratch(big), scratch(grid), scratch((7,) + grid),
            scratch((2, comps, depth, span)), scratch((depth * width, 128)),
            scratch(grid), scratch(grid), scratch(grid), scratch(grid), scratch(grid),
            pltpu.VMEM((2, comps * TILE, comps * TILE), BF16),
            scratch((comps, comps)),
            pltpu.SMEM((comps,), F32), pltpu.SMEM((comps,), F32),
            pltpu.SMEM(two_phase.shape, jnp.int32),
            scratch((width, span)),
            scratch(grid), scratch(grid), scratch(grid), scratch(grid), scratch(grid),
            scratch((7,) + grid),
            scratch((2, depth, span)), scratch((128, depth * width)),
            scratch((2, FIELDS, depth, span)), scratch((2, FIELDS, depth, span)),
            scratch((2, YROWS, depth * width)), scratch((2, YROWS, depth * width)),
            scratch((2, depth, span)), scratch((2, depth, span)),
            scratch((TILE, depth * width)), scratch((2, TILE, depth * width)),
            dma((11,)), dma((4,)), dma((4,)), dma((4,)), dma((4,)),
        ],
        compiler_params=pltpu.CompilerParams(
            collective_id=0, has_side_effects=True, vmem_limit_bytes=VMEM_BYTES
        ),
    )(
        *(
            pltpu.with_memory_space_constraint(value, pltpu.HBM)
            for value in (
                pressure, composition, mass_old, pore_volume, trans_x, trans_y, trans_z,
                volatility, pressure_slope, mixing, two_phase,
            )
        )
    )
    return pl.pallas_call(
        write_kernel,
        name="write",
        out_shape=(array(big), array(grid)),
        in_specs=[local] * 2,
        out_specs=(anywhere, anywhere),
        scratch_shapes=[dma((comps + 1,))],
        compiler_params=pltpu.CompilerParams(vmem_limit_bytes=8 << 20),
    )(out, newp)


def solution(mesh):
    placed = (
        P(None, "areal", "layer"),
        P(None, None, "areal", "layer"),
        P(None, None, "areal", "layer"),
        P(None, "areal", "layer"),
        P(None, "areal", "layer"),
        P(None, "areal", "layer"),
        P(None, "areal", "layer"),
        P(),
        P(),
        P(),
        P(None, "areal"),
    )
    return jax.shard_map(
        on_device,
        mesh=mesh,
        in_specs=placed,
        out_specs=(P(None, None, "areal", "layer"), P(None, "areal", "layer")),
        check_vma=False,
    )
```

```python
import functools

import jax
import jax.numpy as jnp
from jax import lax
from jax.experimental import pallas as pl
from jax.experimental.pallas import tpu as pltpu
from jax.sharding import PartitionSpec as P

SS_ITERS = 3
RR_ITERS = 3
light_count = 4
compress = 0.2
F32 = jnp.float32
BF16 = jnp.bfloat16
MESH = pl.DeviceIdType.MESH
TILE = 8
FIELDS = 12
YROWS = 16
UNROLL = 8
VMEM_BYTES = 24 << 20


def total_of(values):
    return functools.reduce(lambda a, b: a + b, values)


def split_matrix(mix, comps):
    size = comps * TILE
    rows = lax.broadcasted_iota(jnp.int32, (size, comps), 0) // TILE
    cols = lax.broadcasted_iota(jnp.int32, (size, comps), 1)
    pick = (rows == cols).astype(F32)
    wide = lax.dot_general(
        jnp.dot(pick, mix, precision=lax.Precision.HIGHEST, preferred_element_type=F32),
        pick,
        (((1,), (1,)), ((), ())),
        precision=lax.Precision.HIGHEST,
        preferred_element_type=F32,
    )
    a = lax.broadcasted_iota(jnp.int32, (size, size), 0) % TILE
    b = lax.broadcasted_iota(jnp.int32, (size, size), 1) % TILE
    full = jnp.where(a == b, 2.0 * wide, 0.0)
    high = full.astype(BF16)
    return high, (full - high.astype(F32)).astype(BF16)


def mixed(w_ref, parts):
    stack = jnp.concatenate(parts, axis=0)
    high = stack.astype(BF16)
    low = (stack - high.astype(F32)).astype(BF16)
    out = (
        jnp.dot(w_ref[0], high, preferred_element_type=F32)
        + jnp.dot(w_ref[1], high, preferred_element_type=F32)
        + jnp.dot(w_ref[0], low, preferred_element_type=F32)
    )
    return [out[i * TILE : (i + 1) * TILE] for i in range(len(parts))]


def flash(feed, log_p, half_vol, half_slope, w_ref):
    comps = len(feed)
    base = [half_vol[i] - half_slope[i] * log_p for i in range(comps)]
    half_log = base
    moved = None
    for outer in range(SS_ITERS):
        if outer:
            pulled = mixed(w_ref, moved)
            half_log = [base[i] - 0.5 * jnp.tanh(pulled[i]) for i in range(comps)]
        q = [jnp.tanh(v) for v in half_log]
        h = [1.0 / v for v in q]
        centre = None
        for inner in range(RR_ITERS):
            if inner:
                q = [1.0 / (h[i] + centre) for i in range(comps)]
            fq = [feed[i] * q[i] for i in range(comps)]
            step = total_of(fq) / total_of([fq[i] * q[i] for i in range(comps)])
            centre = jnp.clip(step if centre is None else centre + step, -1.0, 1.0)
        moved = [feed[i] * (1.0 / (h[i] + centre)) for i in range(comps)]
    low = 1.0 - centre
    high = 1.0 + centre
    low = 0.25 * (low * low)
    high = high * high
    outer_sum, outer_diff = low + high, high - low
    return [moved[i] * (outer_sum * h[i] + outer_diff) for i in range(comps)]


def flash_kernel(
    comps,
    p_hbm, comp_hbm, mass_hbm, pv_hbm, tx_hbm, ty_hbm, tz_hbm, vol_hbm, slope_hbm, mix_hbm, two_hbm,
    out, newp,
    comp, mass, mob, pvi, grads, xmob, ymob, p, pv, tx, ty, tz, w_ref, mix, vol, slope, two, flags,
    msum, fsum, first, rest, rdiag, coup, mxh, myh,
    xsend, xrecv, ysend, yrecv, fxsend, fxrecv, fxend, fysend, fyrecv,
    in_sem, send_sem, recv_sem, send2_sem, recv2_sem,
):
    depth, width, span = p.shape
    here_a = lax.axis_index("areal")
    here_l = lax.axis_index("layer")
    na = lax.axis_size("areal")
    nl = lax.axis_size("layer")
    xm = (lax.rem(here_a + na - 1, na), here_l)
    xp = (lax.rem(here_a + 1, na), here_l)
    ym = (here_a, lax.rem(here_l + nl - 1, nl))
    yp = (here_a, lax.rem(here_l + 1, nl))

    loads = [
        pltpu.make_async_copy(src, dst, in_sem.at[i])
        for i, (src, dst) in enumerate(
            [
                (mix_hbm, mix), (vol_hbm, vol), (slope_hbm, slope), (two_hbm, two),
                (comp_hbm, comp), (p_hbm, p), (tx_hbm, tx), (ty_hbm, ty),
                (mass_hbm, mass), (pv_hbm, pv), (tz_hbm, tz),
            ]
        )
    ]
    for load in loads:
        load.start()
    barrier = pltpu.get_barrier_semaphore()
    there = (here_a > 0, here_a < na - 1, here_l > 0, here_l < nl - 1)

    def when_there(actions, which=(0, 1, 2, 3)):
        for i, action in zip(which, actions):
            pl.when(there[i])(action)

    def finish(sends, which):
        when_there([sends[i].wait_send for i in which], which)
        when_there([sends[i ^ 1].wait_recv for i in which], which)

    when_there(
        functools.partial(
            pl.semaphore_signal, barrier, inc=1, device_id=device, device_id_type=MESH
        )
        for device in (xm, xp, ym, yp)
    )
    for load in loads[:4]:
        load.wait()
    w_ref[0], w_ref[1] = split_matrix(mix[...], comps)
    half_vol = [(0.5 if i < light_count else -0.5) * vol[i] for i in range(comps)]
    half_slope = [0.5 * slope[i] for i in range(comps)]
    bricks = two.shape[1]
    brick_of = lax.broadcasted_iota(jnp.int32, (width, span), 0) // (width // bricks)
    flag = jnp.zeros((width, span), F32)
    for b in range(bricks):
        flag = jnp.where(brick_of == b, two[here_l, b].astype(F32), flag)
    flags[...] = flag
    for load in loads[4:8]:
        load.wait()

    lane = lax.broadcasted_iota(jnp.int32, (width, 128), 1)

    def pack(z, carry):
        packed = jnp.zeros((width, 128), F32)
        for side, cut in ((0, 0), (1, span - 128)):
            source = 0 if side == 0 else 127
            for k in range(FIELDS):
                if k < comps:
                    value = comp[k, z, :, cut : cut + 128]
                elif k == comps:
                    value = p[z, :, cut : cut + 128]
                elif k == comps + 1:
                    value = ty[z, :, cut : cut + 128]
                else:
                    value = flags[:, cut : cut + 128]
                target = side * YROWS + k
                moved = pltpu.roll(value, (target - source) % 128, 1)
                packed = jnp.where(lane == target, moved, packed)
        ymob[pl.ds(pl.multiple_of(z * width, width), width), :] = packed
        for side, row in ((0, 0), (1, width - 1)):
            for k in range(comps):
                xsend[side, k, pl.ds(z, 1), :] = comp[k, z, row : row + 1, :]
            xsend[side, comps, pl.ds(z, 1), :] = p[z, row : row + 1, :]
            xsend[side, comps + 1, pl.ds(z, 1), :] = tx[z, row : row + 1, :]
            xsend[side, comps + 2, pl.ds(z, 1), :] = flags[row : row + 1, :]
        return carry

    lax.fori_loop(0, depth, pack, 0, unroll=4)
    turned = jnp.transpose(ymob[...])
    ysend[0] = turned[:YROWS]
    ysend[1] = turned[YROWS : 2 * YROWS]
    sends = [
        pltpu.make_async_remote_copy(
            src_ref=src, dst_ref=dst, send_sem=send_sem.at[i], recv_sem=recv_sem.at[i],
            device_id=device, device_id_type=MESH,
        )
        for i, (src, dst, device) in enumerate(
            [
                (xsend.at[0], xrecv.at[1], xm), (xsend.at[1], xrecv.at[0], xp),
                (ysend.at[0], yrecv.at[1], ym), (ysend.at[1], yrecv.at[0], yp),
            ]
        )
    ]

    for exists, slot in zip(there, (xrecv.at[0], xrecv.at[1], yrecv.at[0], yrecv.at[1])):

        @pl.when(jnp.logical_not(exists))
        def _(slot=slot):
            slot[...] = jnp.ones(slot.shape, F32)

    def cells(values, pressure, flagged):
        total = total_of(values)
        inverse = 1.0 / total
        feed = [v * inverse for v in values]
        moved = flash(feed, jnp.log(pressure), half_vol, half_slope, w_ref)
        return inverse, total * inverse, [
            jnp.where(flagged > 0.0, moved[i], feed[i]) for i in range(comps)
        ]

    blocks = width // TILE
    chunks = blocks * depth // UNROLL

    def block(step):
        inner = step // (2 * depth)
        pair = step % (2 * depth)
        z = pair // 2
        place = (1 - inner) * (blocks - 1) * (pair % 2) + inner * (1 + pair % 2)
        rows = pl.ds(pl.multiple_of(place * TILE, TILE), TILE)
        values = [comp[i, z, rows, :] for i in range(comps)]
        inverse, whole, found = cells(values, p[z, rows, :], flags[rows, :])
        pvi[z, rows, :] = inverse
        fsum[z, rows, :] = whole
        for i in range(comps):
            mob[i, z, rows, :] = found[i]
        msum[z, rows, :] = total_of(found)

    def chunk(index, carry):
        def body(step, inner):
            block(index * UNROLL + step)
            return inner

        return lax.fori_loop(0, UNROLL, body, carry, unroll=True)

    early = 1 - (here_a // 2) % 2
    edge_chunks = chunks // 2
    send_after = early * edge_chunks
    share_after = edge_chunks + early * (chunks - edge_chunks)
    lax.fori_loop(0, send_after, chunk, 0)
    pl.semaphore_wait(barrier, total_of([exists.astype(jnp.int32) for exists in there]))
    when_there(send.start for send in sends)
    lax.fori_loop(send_after, share_after, chunk, 0)
    for load in loads[8:]:
        load.wait()

    finish(sends, (2, 3))
    sub = lax.broadcasted_iota(jnp.int32, (TILE, span), 0)

    def both(k):
        return jnp.where(sub == 0, yrecv[0, k : k + 1, :], yrecv[1, k : k + 1, :])

    _, _, found = cells([both(k) for k in range(comps)], both(comps), both(comps + 2))
    together = found + [total_of(found), both(comps), both(comps + 1)]
    for side in range(2):
        for k, value in enumerate(together):
            myh[side * YROWS + k : side * YROWS + k + 1, :] = value[side : side + 1, :]
    ymob[...] = jnp.transpose(myh[...])

    row_id = lax.broadcasted_iota(jnp.int32, (width, span), 0)
    lane_id = lax.broadcasted_iota(jnp.int32, (width, span), 1)
    has_xm = (here_a > 0).astype(F32)
    has_xp = (here_a < na - 1).astype(F32)
    has_ym = (here_l > 0).astype(F32)
    has_yp = (here_l < nl - 1).astype(F32)

    def before_x(value, edge):
        return jnp.where(row_id == 0, edge, pltpu.roll(value, 1, 0))

    def after_x(value, edge):
        return jnp.where(row_id == width - 1, edge, pltpu.roll(value, width - 1, 0))

    def before_y(value, edge):
        return jnp.where(lane_id == 0, edge, pltpu.roll(value, 1, 1))

    def after_y(value, edge):
        return jnp.where(lane_id == span - 1, edge, pltpu.roll(value, span - 1, 1))

    edge_lane = lax.broadcasted_iota(jnp.int32, (depth, span), 1)
    level_id = lax.broadcasted_iota(jnp.int32, (depth, span), 0)

    def row_of(ref, r):
        return ref[:, r, :]

    for side, row, inside in ((0, 0, 1), (1, width - 1, width - 2)):
        edge = ymob[pl.ds(row, depth, stride=width), :]

        def near_y(value, k, edge=edge):
            return (
                jnp.where(
                    edge_lane == span - 1,
                    edge[:, YROWS + k : YROWS + k + 1],
                    pltpu.roll(value, span - 1, 1),
                ),
                jnp.where(edge_lane == 0, edge[:, k : k + 1], pltpu.roll(value, 1, 1)),
            )

        here_p, here_m = row_of(p, row), row_of(msum, row)
        t_y, t_z = row_of(ty, row), row_of(tz, row)
        strength = [
            jnp.where(level_id == depth - 1, 0.0, t_z),
            jnp.where(level_id == 0, 0.0, pltpu.roll(t_z, 1, 0)),
            row_of(tx, min(row, inside)),
            jnp.where(edge_lane == span - 1, has_yp * t_y, t_y),
            jnp.where(
                edge_lane == 0, has_ym * edge[:, comps + 2 : comps + 3], pltpu.roll(t_y, 1, 1)
            ),
        ]
        near_p = [
            pltpu.roll(here_p, depth - 1, 0), pltpu.roll(here_p, 1, 0), row_of(p, inside),
            *near_y(here_p, comps + 1),
        ]
        near_m = [
            pltpu.roll(here_m, depth - 1, 0), pltpu.roll(here_m, 1, 0), row_of(msum, inside),
            *near_y(here_m, comps),
        ]
        volume = row_of(pv, row)
        balance = volume * row_of(fsum, row) - total_of(
            [mass[i, :, row, :] for i in range(comps)]
        )
        diagonal = compress * volume
        for f in range(5):
            link = 2.0 * strength[f] * (here_m + near_m[f])
            balance = balance + link * (here_p - near_p[f])
            diagonal = diagonal + link
        fxsend[side, 0] = balance
        fxsend[side, 1] = diagonal
    shares = [
        pltpu.make_async_remote_copy(
            src_ref=src, dst_ref=dst, send_sem=send2_sem.at[i], recv_sem=recv2_sem.at[i],
            device_id=device, device_id_type=MESH,
        )
        for i, (src, dst, device) in enumerate(
            [
                (fxsend.at[0], fxrecv.at[1], xm), (fxsend.at[1], fxrecv.at[0], xp),
                (fysend, fyrecv.at[1], ym), (fysend, fyrecv.at[0], yp),
            ]
        )
    ]
    when_there([share.start for share in shares[:2]])
    lax.fori_loop(share_after, chunks, chunk, 0)

    finish(sends, (0, 1))
    for side in range(2):
        values = [xrecv[side, k] for k in range(comps)]
        _, _, found = cells(values, xrecv[side, comps], xrecv[side, comps + 2])
        for i in range(comps):
            xmob[side, i] = found[i]
        mxh[side] = total_of(found)

    def faces(z, carry):
        up = jnp.minimum(z + 1, depth - 1)
        down = jnp.maximum(z - 1, 0)
        zrow = pl.ds(z, 1)
        yrow = pl.ds(pl.multiple_of(z * width, width), width)
        here_p, here_m = p[z], msum[z]
        edge = ymob[yrow, :]
        em = [edge[:, k : k + 1] for k in (comps, comps + 1, comps + 2)]
        ep = [edge[:, YROWS + k : YROWS + k + 1] for k in (comps, comps + 1)]
        t_x, t_y = tx[z], ty[z]
        strength = [
            tz[z] * (z < depth - 1).astype(F32),
            tz[down] * (z > 0).astype(F32),
            jnp.where(row_id == width - 1, has_xp * t_x, t_x),
            before_x(t_x, has_xm * xrecv[0, comps + 1, zrow, :]),
            jnp.where(lane_id == span - 1, has_yp * t_y, t_y),
            before_y(t_y, has_ym * em[2]),
        ]
        near_p = [
            p[up], p[down],
            after_x(here_p, xrecv[1, comps, zrow, :]), before_x(here_p, xrecv[0, comps, zrow, :]),
            after_y(here_p, ep[1]), before_y(here_p, em[1]),
        ]
        near_m = [
            msum[up], msum[down],
            after_x(here_m, mxh[1, zrow, :]), before_x(here_m, mxh[0, zrow, :]),
            after_y(here_m, ep[0]), before_y(here_m, em[0]),
        ]
        volume = pv[z]
        balance = volume * fsum[z] - total_of([mass[i, z] for i in range(comps)])
        diagonal = compress * volume
        centre = None
        for f in range(6):
            twice = 2.0 * strength[f]
            fall = here_p - near_p[f]
            link = twice * (here_m + near_m[f])
            slope_f = twice * fall
            balance = balance + link * fall
            diagonal = diagonal + link
            grads[f, z] = slope_f
            coup[f, z] = link
            centre = slope_f if centre is None else centre + slope_f
        grads[6, z] = centre
        inverse = 1.0 / diagonal
        update = -balance * inverse
        first[z] = update
        rest[z] = -balance
        rdiag[z] = inverse
        pvi[z] = volume * pvi[z]
        left = update[:, 0:128]
        right = pltpu.roll(update[:, span - 128 : span], 2, 1)
        coup[6, z, :, 0:128] = jnp.where(lane == 0, left, right)
        return carry

    lax.fori_loop(0, depth, faces, 0, unroll=2)
    stacked = coup[6, :, :, 0:128].reshape(depth * width, 128)
    fysend[...] = jnp.transpose(stacked)[:TILE]
    when_there([share.start for share in shares[2:]], (2, 3))

    def level(z, i):
        up = jnp.minimum(z + 1, depth - 1)
        down = jnp.maximum(z - 1, 0)
        zrow = pl.ds(z, 1)
        here = mob[i, z]
        edge = ymob[pl.ds(pl.multiple_of(z * width, width), width), :]
        near = [
            mob[i, up], mob[i, down],
            after_x(here, xmob[1, i, zrow, :]), before_x(here, xmob[0, i, zrow, :]),
            after_y(here, edge[:, YROWS + i : YROWS + i + 1]), before_y(here, edge[:, i : i + 1]),
        ]
        value = pvi[z] * comp[i, z] - mass[i, z] + grads[6, z] * here
        for f in range(6):
            value = value + grads[f, z] * near[f]
        out[i, z] = value

    for i in range(comps):

        def body(z, carry, i=i):
            level(z, i)
            return carry

        lax.fori_loop(0, depth, body, 0, unroll=8)
    finish(shares, (0, 1, 2, 3))
    for exists, slot in zip(there, (fxrecv.at[0], fxrecv.at[1], fyrecv.at[0], fyrecv.at[1])):

        @pl.when(jnp.logical_not(exists))
        def _(slot=slot):
            slot[...] = jnp.ones(slot.shape, F32)

    for side, row, exists in ((0, 0, has_xm), (1, width - 1, has_xp)):
        face = xrecv[0, comps + 1] if side == 0 else row_of(tx, row)
        link = 2.0 * exists * face * (mxh[side] + row_of(msum, row))
        fall = xrecv[side, comps] - row_of(p, row)
        fxend[side] = -(fxrecv[side, 0] + link * fall) / (fxrecv[side, 1] + link)

    myh[0:1, :] = fyrecv[0, 1:2, :]
    myh[1:2, :] = fyrecv[1, 0:1, :]
    coup[6, :, :, 0:128] = jnp.transpose(myh[...]).reshape(depth, width, 128)

    def update(z, carry):
        up = jnp.minimum(z + 1, depth - 1)
        down = jnp.maximum(z - 1, 0)
        zrow = pl.ds(z, 1)
        value = first[z]
        edge = coup[6, z, :, 0:128]
        near = [
            first[up], first[down],
            after_x(value, fxend[1, zrow, :]), before_x(value, fxend[0, zrow, :]),
            after_y(value, edge[:, 1:2]), before_y(value, edge[:, 0:1]),
        ]
        gathered = rest[z]
        for f in range(6):
            gathered = gathered + coup[f, z] * near[f]
        newp[z] = p[z] + gathered * rdiag[z]
        return carry

    lax.fori_loop(0, depth, update, 0, unroll=4)


def write_kernel(value, newp, out_hbm, newp_hbm, sem):
    copies = [
        pltpu.make_async_copy(src, dst, sem.at[i])
        for i, (src, dst) in enumerate(
            [(value, out_hbm), (newp, newp_hbm)]
        )
    ]
    for copy in copies:
        copy.start()
    for copy in copies:
        copy.wait()


def on_device(
    pressure, composition, mass_old, pore_volume, trans_x, trans_y, trans_z,
    volatility, pressure_slope, mixing, two_phase,
):
    comps = composition.shape[0]
    grid = pressure.shape
    depth, width, span = grid
    big = (comps,) + grid
    anywhere = pl.BlockSpec(memory_space=pltpu.HBM)
    local = pl.BlockSpec(memory_space=pltpu.VMEM)
    dma = pltpu.SemaphoreType.DMA

    def array(shape):
        return jax.ShapeDtypeStruct(shape, F32)

    def scratch(shape):
        return pltpu.VMEM(shape, F32)

    out, newp = pl.pallas_call(
        functools.partial(flash_kernel, comps),
        name="flash",
        out_shape=(array(big), array(grid)),
        in_specs=[anywhere] * 11,
        out_specs=(local,) * 2,
        scratch_shapes=[
            scratch(big), scratch(big), scratch(big), scratch(grid), scratch((7,) + grid),
            scratch((2, comps, depth, span)), scratch((depth * width, 128)),
            scratch(grid), scratch(grid), scratch(grid), scratch(grid), scratch(grid),
            pltpu.VMEM((2, comps * TILE, comps * TILE), BF16),
            scratch((comps, comps)),
            pltpu.SMEM((comps,), F32), pltpu.SMEM((comps,), F32),
            pltpu.SMEM(two_phase.shape, jnp.int32),
            scratch((width, span)),
            scratch(grid), scratch(grid), scratch(grid), scratch(grid), scratch(grid),
            scratch((7,) + grid),
            scratch((2, depth, span)), scratch((128, depth * width)),
            scratch((2, FIELDS, depth, span)), scratch((2, FIELDS, depth, span)),
            scratch((2, YROWS, depth * width)), scratch((2, YROWS, depth * width)),
            scratch((2, 2, depth, span)), scratch((2, 2, depth, span)), scratch((2, depth, span)),
            scratch((TILE, depth * width)), scratch((2, TILE, depth * width)),
            dma((11,)), dma((4,)), dma((4,)), dma((4,)), dma((4,)),
        ],
        compiler_params=pltpu.CompilerParams(
            collective_id=0, has_side_effects=True, vmem_limit_bytes=VMEM_BYTES
        ),
    )(
        *(
            pltpu.with_memory_space_constraint(value, pltpu.HBM)
            for value in (
                pressure, composition, mass_old, pore_volume, trans_x, trans_y, trans_z,
                volatility, pressure_slope, mixing, two_phase,
            )
        )
    )
    return pl.pallas_call(
        write_kernel,
        name="write",
        out_shape=(array(big), array(grid)),
        in_specs=[local] * 2,
        out_specs=(anywhere, anywhere),
        scratch_shapes=[dma((comps + 1,))],
        compiler_params=pltpu.CompilerParams(vmem_limit_bytes=8 << 20),
    )(out, newp)


def solution(mesh):
    placed = (
        P(None, "areal", "layer"),
        P(None, None, "areal", "layer"),
        P(None, None, "areal", "layer"),
        P(None, "areal", "layer"),
        P(None, "areal", "layer"),
        P(None, "areal", "layer"),
        P(None, "areal", "layer"),
        P(),
        P(),
        P(),
        P(None, "areal"),
    )
    return jax.shard_map(
        on_device,
        mesh=mesh,
        in_specs=placed,
        out_specs=(P(None, None, "areal", "layer"), P(None, "areal", "layer")),
        check_vma=False,
    )
```

```python
import functools

import jax
import jax.numpy as jnp
from jax import lax
from jax.experimental import pallas as pl
from jax.experimental.pallas import tpu as pltpu
from jax.sharding import PartitionSpec as P

SS_ITERS = 3
RR_ITERS = 3
light_count = 4
compress = 0.2
F32 = jnp.float32
BF16 = jnp.bfloat16
MESH = pl.DeviceIdType.MESH
TILE = 8
FIELDS = 12
YROWS = 16
UNROLL = 8
VMEM_BYTES = 24 << 20


def total_of(values):
    return functools.reduce(lambda a, b: a + b, values)


def split_matrix(mix, comps):
    size = comps * TILE
    rows = lax.broadcasted_iota(jnp.int32, (size, comps), 0) // TILE
    cols = lax.broadcasted_iota(jnp.int32, (size, comps), 1)
    pick = (rows == cols).astype(F32)
    wide = lax.dot_general(
        jnp.dot(pick, mix, precision=lax.Precision.HIGHEST, preferred_element_type=F32),
        pick,
        (((1,), (1,)), ((), ())),
        precision=lax.Precision.HIGHEST,
        preferred_element_type=F32,
    )
    a = lax.broadcasted_iota(jnp.int32, (size, size), 0) % TILE
    b = lax.broadcasted_iota(jnp.int32, (size, size), 1) % TILE
    full = jnp.where(a == b, 2.0 * wide, 0.0)
    high = full.astype(BF16)
    return high, (full - high.astype(F32)).astype(BF16)


def mixed(w_ref, parts):
    stack = jnp.concatenate(parts, axis=0)
    high = stack.astype(BF16)
    low = (stack - high.astype(F32)).astype(BF16)
    out = (
        jnp.dot(w_ref[0], high, preferred_element_type=F32)
        + jnp.dot(w_ref[1], high, preferred_element_type=F32)
        + jnp.dot(w_ref[0], low, preferred_element_type=F32)
    )
    return [out[i * TILE : (i + 1) * TILE] for i in range(len(parts))]


def flash(feed, log_p, half_vol, half_slope, w_ref):
    comps = len(feed)
    base = [half_vol[i] - half_slope[i] * log_p for i in range(comps)]
    half_log = base
    moved = None
    for outer in range(SS_ITERS):
        if outer:
            pulled = mixed(w_ref, moved)
            half_log = [base[i] - 0.5 * jnp.tanh(pulled[i]) for i in range(comps)]
        q = [jnp.tanh(v) for v in half_log]
        h = [1.0 / v for v in q]
        centre = None
        for inner in range(RR_ITERS):
            if inner:
                q = [1.0 / (h[i] + centre) for i in range(comps)]
            fq = [feed[i] * q[i] for i in range(comps)]
            step = total_of(fq) / total_of([fq[i] * q[i] for i in range(comps)])
            centre = jnp.clip(step if centre is None else centre + step, -1.0, 1.0)
        moved = [feed[i] * (1.0 / (h[i] + centre)) for i in range(comps)]
    low = 1.0 - centre
    high = 1.0 + centre
    low = 0.25 * (low * low)
    high = high * high
    outer_sum, outer_diff = low + high, high - low
    return [moved[i] * (outer_sum * h[i] + outer_diff) for i in range(comps)]


def flash_kernel(
    comps,
    p_hbm, comp_hbm, mass_hbm, pv_hbm, tx_hbm, ty_hbm, tz_hbm, vol_hbm, slope_hbm, mix_hbm, two_hbm,
    out, newp,
    comp, mass, mob, pvi, grads, xmob, ymob, p, pv, tx, ty, tz, w_ref, mix, vol, slope, two, flags,
    msum, fsum, first, rest, rdiag, coup, mxh, myh,
    xsend, xrecv, ysend, yrecv, fxsend, fxrecv, fxend, fysend, fyrecv,
    in_sem, send_sem, recv_sem, send2_sem, recv2_sem,
):
    depth, width, span = p.shape
    here_a = lax.axis_index("areal")
    here_l = lax.axis_index("layer")
    na = lax.axis_size("areal")
    nl = lax.axis_size("layer")
    xm = (lax.rem(here_a + na - 1, na), here_l)
    xp = (lax.rem(here_a + 1, na), here_l)
    ym = (here_a, lax.rem(here_l + nl - 1, nl))
    yp = (here_a, lax.rem(here_l + 1, nl))

    low, high = pl.ds(0, TILE), pl.ds(width - TILE, TILE)
    inner = pl.ds(TILE, width - 2 * TILE)
    loads = [
        pltpu.make_async_copy(src, dst, in_sem.at[i])
        for i, (src, dst) in enumerate(
            [
                (two_hbm, two),
                (comp_hbm.at[:, :, low, :], comp.at[:, :, low, :]),
                (comp_hbm.at[:, :, high, :], comp.at[:, :, high, :]),
                (p_hbm, p), (tx_hbm, tx),
                (mix_hbm, mix), (vol_hbm, vol), (slope_hbm, slope),
                (comp_hbm.at[:, :, inner, :], comp.at[:, :, inner, :]), (ty_hbm, ty),
                (mass_hbm, mass), (pv_hbm, pv), (tz_hbm, tz),
            ]
        )
    ]
    for load in loads:
        load.start()
    barrier = pltpu.get_barrier_semaphore()
    there = (here_a > 0, here_a < na - 1, here_l > 0, here_l < nl - 1)

    def when_there(actions, which=(0, 1, 2, 3)):
        for i, action in zip(which, actions):
            pl.when(there[i])(action)

    def finish(sends, which):
        when_there([sends[i].wait_send for i in which], which)
        when_there([sends[i ^ 1].wait_recv for i in which], which)

    when_there(
        functools.partial(
            pl.semaphore_signal, barrier, inc=1, device_id=device, device_id_type=MESH
        )
        for device in (xm, xp, ym, yp)
    )
    for load in loads[:5]:
        load.wait()
    bricks = two.shape[1]
    brick_of = lax.broadcasted_iota(jnp.int32, (width, span), 0) // (width // bricks)
    flag = jnp.zeros((width, span), F32)
    for b in range(bricks):
        flag = jnp.where(brick_of == b, two[here_l, b].astype(F32), flag)
    flags[...] = flag
    def pack_x(z, carry):
        for side, row in ((0, 0), (1, width - 1)):
            for k in range(comps):
                xsend[side, k, pl.ds(z, 1), :] = comp[k, z, row : row + 1, :]
            xsend[side, comps, pl.ds(z, 1), :] = p[z, row : row + 1, :]
            xsend[side, comps + 1, pl.ds(z, 1), :] = tx[z, row : row + 1, :]
            xsend[side, comps + 2, pl.ds(z, 1), :] = flags[row : row + 1, :]
        return carry

    lax.fori_loop(0, depth, pack_x, 0, unroll=4)
    lane = lax.broadcasted_iota(jnp.int32, (width, 128), 1)
    sends = [
        pltpu.make_async_remote_copy(
            src_ref=src, dst_ref=dst, send_sem=send_sem.at[i], recv_sem=recv_sem.at[i],
            device_id=device, device_id_type=MESH,
        )
        for i, (src, dst, device) in enumerate(
            [
                (xsend.at[0], xrecv.at[1], xm), (xsend.at[1], xrecv.at[0], xp),
                (ysend.at[0], yrecv.at[1], ym), (ysend.at[1], yrecv.at[0], yp),
            ]
        )
    ]

    early = 1 - (here_a // 2) % 2

    def send_x():
        pl.semaphore_wait(barrier, total_of([exists.astype(jnp.int32) for exists in there]))
        when_there([send.start for send in sends[:2]])

    pl.when(early == 0)(send_x)
    for load in loads[5:8]:
        load.wait()
    w_ref[0], w_ref[1] = split_matrix(mix[...], comps)
    half_vol = [(0.5 if i < light_count else -0.5) * vol[i] for i in range(comps)]
    half_slope = [0.5 * slope[i] for i in range(comps)]
    for exists, slot in zip(there, (xrecv.at[0], xrecv.at[1], yrecv.at[0], yrecv.at[1])):

        @pl.when(jnp.logical_not(exists))
        def _(slot=slot):
            slot[...] = jnp.ones(slot.shape, F32)

    def cells(values, pressure, flagged):
        total = total_of(values)
        inverse = 1.0 / total
        feed = [v * inverse for v in values]
        moved = flash(feed, jnp.log(pressure), half_vol, half_slope, w_ref)
        return inverse, total * inverse, [
            jnp.where(flagged > 0.0, moved[i], feed[i]) for i in range(comps)
        ]

    blocks = width // TILE
    chunks = blocks * depth // UNROLL

    def block(step):
        inner = step // (2 * depth)
        pair = step % (2 * depth)
        z = pair // 2
        place = (1 - inner) * (blocks - 1) * (pair % 2) + inner * (1 + pair % 2)
        rows = pl.ds(pl.multiple_of(place * TILE, TILE), TILE)
        values = [comp[i, z, rows, :] for i in range(comps)]
        inverse, whole, found = cells(values, p[z, rows, :], flags[rows, :])
        pvi[z, rows, :] = inverse
        fsum[z, rows, :] = whole
        for i in range(comps):
            mob[i, z, rows, :] = found[i]
        msum[z, rows, :] = total_of(found)

    def chunk(index, carry):
        def body(step, inner):
            block(index * UNROLL + step)
            return inner

        return lax.fori_loop(0, UNROLL, body, carry, unroll=True)

    edge_chunks = chunks // 2
    send_after = early * edge_chunks
    share_after = edge_chunks + early * (chunks - edge_chunks)
    lax.fori_loop(0, send_after, chunk, 0)
    pl.when(early == 1)(send_x)
    for load in loads[8:10]:
        load.wait()

    def pack_y(z, carry):
        packed = jnp.zeros((width, 128), F32)
        for side, cut in ((0, 0), (1, span - 128)):
            source = 0 if side == 0 else 127
            for k in range(FIELDS):
                if k < comps:
                    value = comp[k, z, :, cut : cut + 128]
                elif k == comps:
                    value = p[z, :, cut : cut + 128]
                elif k == comps + 1:
                    value = ty[z, :, cut : cut + 128]
                else:
                    value = flags[:, cut : cut + 128]
                target = side * YROWS + k
                moved = pltpu.roll(value, (target - source) % 128, 1)
                packed = jnp.where(lane == target, moved, packed)
        ymob[pl.ds(pl.multiple_of(z * width, width), width), :] = packed
        return carry

    lax.fori_loop(0, depth, pack_y, 0, unroll=4)
    turned = jnp.transpose(ymob[...])
    ysend[0] = turned[:YROWS]
    ysend[1] = turned[YROWS : 2 * YROWS]
    when_there([send.start for send in sends[2:]], (2, 3))
    lax.fori_loop(send_after, share_after, chunk, 0)
    for load in loads[10:]:
        load.wait()

    finish(sends, (2, 3))
    sub = lax.broadcasted_iota(jnp.int32, (TILE, span), 0)

    def both(k):
        return jnp.where(sub == 0, yrecv[0, k : k + 1, :], yrecv[1, k : k + 1, :])

    _, _, found = cells([both(k) for k in range(comps)], both(comps), both(comps + 2))
    together = found + [total_of(found), both(comps), both(comps + 1)]
    for side in range(2):
        for k, value in enumerate(together):
            myh[side * YROWS + k : side * YROWS + k + 1, :] = value[side : side + 1, :]
    ymob[...] = jnp.transpose(myh[...])

    row_id = lax.broadcasted_iota(jnp.int32, (width, span), 0)
    lane_id = lax.broadcasted_iota(jnp.int32, (width, span), 1)
    has_xm = (here_a > 0).astype(F32)
    has_xp = (here_a < na - 1).astype(F32)
    has_ym = (here_l > 0).astype(F32)
    has_yp = (here_l < nl - 1).astype(F32)

    def before_x(value, edge):
        return jnp.where(row_id == 0, edge, pltpu.roll(value, 1, 0))

    def after_x(value, edge):
        return jnp.where(row_id == width - 1, edge, pltpu.roll(value, width - 1, 0))

    def before_y(value, edge):
        return jnp.where(lane_id == 0, edge, pltpu.roll(value, 1, 1))

    def after_y(value, edge):
        return jnp.where(lane_id == span - 1, edge, pltpu.roll(value, span - 1, 1))

    edge_lane = lax.broadcasted_iota(jnp.int32, (depth, span), 1)
    level_id = lax.broadcasted_iota(jnp.int32, (depth, span), 0)

    def row_of(ref, r):
        return ref[:, r, :]

    for side, row, inside in ((0, 0, 1), (1, width - 1, width - 2)):
        edge = ymob[pl.ds(row, depth, stride=width), :]

        def near_y(value, k, edge=edge):
            return (
                jnp.where(
                    edge_lane == span - 1,
                    edge[:, YROWS + k : YROWS + k + 1],
                    pltpu.roll(value, span - 1, 1),
                ),
                jnp.where(edge_lane == 0, edge[:, k : k + 1], pltpu.roll(value, 1, 1)),
            )

        here_p, here_m = row_of(p, row), row_of(msum, row)
        t_y, t_z = row_of(ty, row), row_of(tz, row)
        strength = [
            jnp.where(level_id == depth - 1, 0.0, t_z),
            jnp.where(level_id == 0, 0.0, pltpu.roll(t_z, 1, 0)),
            row_of(tx, min(row, inside)),
            jnp.where(edge_lane == span - 1, has_yp * t_y, t_y),
            jnp.where(
                edge_lane == 0, has_ym * edge[:, comps + 2 : comps + 3], pltpu.roll(t_y, 1, 1)
            ),
        ]
        near_p = [
            pltpu.roll(here_p, depth - 1, 0), pltpu.roll(here_p, 1, 0), row_of(p, inside),
            *near_y(here_p, comps + 1),
        ]
        near_m = [
            pltpu.roll(here_m, depth - 1, 0), pltpu.roll(here_m, 1, 0), row_of(msum, inside),
            *near_y(here_m, comps),
        ]
        volume = row_of(pv, row)
        balance = volume * row_of(fsum, row) - total_of(
            [mass[i, :, row, :] for i in range(comps)]
        )
        diagonal = compress * volume
        for f in range(5):
            link = 2.0 * strength[f] * (here_m + near_m[f])
            balance = balance + link * (here_p - near_p[f])
            diagonal = diagonal + link
        fxsend[side, 0] = balance
        fxsend[side, 1] = diagonal
    shares = [
        pltpu.make_async_remote_copy(
            src_ref=src, dst_ref=dst, send_sem=send2_sem.at[i], recv_sem=recv2_sem.at[i],
            device_id=device, device_id_type=MESH,
        )
        for i, (src, dst, device) in enumerate(
            [
                (fxsend.at[0], fxrecv.at[1], xm), (fxsend.at[1], fxrecv.at[0], xp),
                (fysend, fyrecv.at[1], ym), (fysend, fyrecv.at[0], yp),
            ]
        )
    ]
    when_there([share.start for share in shares[:2]])
    lax.fori_loop(share_after, chunks, chunk, 0)

    finish(sends, (0, 1))
    for side in range(2):
        values = [xrecv[side, k] for k in range(comps)]
        _, _, found = cells(values, xrecv[side, comps], xrecv[side, comps + 2])
        for i in range(comps):
            xmob[side, i] = found[i]
        mxh[side] = total_of(found)

    def faces(z, carry):
        up = jnp.minimum(z + 1, depth - 1)
        down = jnp.maximum(z - 1, 0)
        zrow = pl.ds(z, 1)
        yrow = pl.ds(pl.multiple_of(z * width, width), width)
        here_p, here_m = p[z], msum[z]
        edge = ymob[yrow, :]
        em = [edge[:, k : k + 1] for k in (comps, comps + 1, comps + 2)]
        ep = [edge[:, YROWS + k : YROWS + k + 1] for k in (comps, comps + 1)]
        t_x, t_y = tx[z], ty[z]
        strength = [
            tz[z] * (z < depth - 1).astype(F32),
            tz[down] * (z > 0).astype(F32),
            jnp.where(row_id == width - 1, has_xp * t_x, t_x),
            before_x(t_x, has_xm * xrecv[0, comps + 1, zrow, :]),
            jnp.where(lane_id == span - 1, has_yp * t_y, t_y),
            before_y(t_y, has_ym * em[2]),
        ]
        near_p = [
            p[up], p[down],
            after_x(here_p, xrecv[1, comps, zrow, :]), before_x(here_p, xrecv[0, comps, zrow, :]),
            after_y(here_p, ep[1]), before_y(here_p, em[1]),
        ]
        near_m = [
            msum[up], msum[down],
            after_x(here_m, mxh[1, zrow, :]), before_x(here_m, mxh[0, zrow, :]),
            after_y(here_m, ep[0]), before_y(here_m, em[0]),
        ]
        volume = pv[z]
        balance = volume * fsum[z] - total_of([mass[i, z] for i in range(comps)])
        diagonal = compress * volume
        centre = None
        for f in range(6):
            twice = 2.0 * strength[f]
            fall = here_p - near_p[f]
            link = twice * (here_m + near_m[f])
            slope_f = twice * fall
            balance = balance + link * fall
            diagonal = diagonal + link
            grads[f, z] = slope_f
            coup[f, z] = link
            centre = slope_f if centre is None else centre + slope_f
        grads[6, z] = centre
        inverse = 1.0 / diagonal
        update = -balance * inverse
        first[z] = update
        rest[z] = -balance
        rdiag[z] = inverse
        pvi[z] = volume * pvi[z]
        left = update[:, 0:128]
        right = pltpu.roll(update[:, span - 128 : span], 2, 1)
        coup[6, z, :, 0:128] = jnp.where(lane == 0, left, right)
        return carry

    lax.fori_loop(0, depth, faces, 0, unroll=4)
    stacked = coup[6, :, :, 0:128].reshape(depth * width, 128)
    fysend[...] = jnp.transpose(stacked)[:TILE]
    when_there([share.start for share in shares[2:]], (2, 3))

    def level(z, i):
        up = jnp.minimum(z + 1, depth - 1)
        down = jnp.maximum(z - 1, 0)
        zrow = pl.ds(z, 1)
        here = mob[i, z]
        edge = ymob[pl.ds(pl.multiple_of(z * width, width), width), :]
        near = [
            mob[i, up], mob[i, down],
            after_x(here, xmob[1, i, zrow, :]), before_x(here, xmob[0, i, zrow, :]),
            after_y(here, edge[:, YROWS + i : YROWS + i + 1]), before_y(here, edge[:, i : i + 1]),
        ]
        value = pvi[z] * comp[i, z] - mass[i, z] + grads[6, z] * here
        for f in range(6):
            value = value + grads[f, z] * near[f]
        out[i, z] = value

    for i in range(comps):

        def body(z, carry, i=i):
            level(z, i)
            return carry

        lax.fori_loop(0, depth, body, 0, unroll=8)
    finish(shares, (0, 1, 2, 3))
    for exists, slot in zip(there, (fxrecv.at[0], fxrecv.at[1], fyrecv.at[0], fyrecv.at[1])):

        @pl.when(jnp.logical_not(exists))
        def _(slot=slot):
            slot[...] = jnp.ones(slot.shape, F32)

    for side, row, exists in ((0, 0, has_xm), (1, width - 1, has_xp)):
        face = xrecv[0, comps + 1] if side == 0 else row_of(tx, row)
        link = 2.0 * exists * face * (mxh[side] + row_of(msum, row))
        fall = xrecv[side, comps] - row_of(p, row)
        fxend[side] = -(fxrecv[side, 0] + link * fall) / (fxrecv[side, 1] + link)

    myh[0:1, :] = fyrecv[0, 1:2, :]
    myh[1:2, :] = fyrecv[1, 0:1, :]
    coup[6, :, :, 0:128] = jnp.transpose(myh[...]).reshape(depth, width, 128)

    def update(z, carry):
        up = jnp.minimum(z + 1, depth - 1)
        down = jnp.maximum(z - 1, 0)
        zrow = pl.ds(z, 1)
        value = first[z]
        edge = coup[6, z, :, 0:128]
        near = [
            first[up], first[down],
            after_x(value, fxend[1, zrow, :]), before_x(value, fxend[0, zrow, :]),
            after_y(value, edge[:, 1:2]), before_y(value, edge[:, 0:1]),
        ]
        gathered = rest[z]
        for f in range(6):
            gathered = gathered + coup[f, z] * near[f]
        newp[z] = p[z] + gathered * rdiag[z]
        return carry

    lax.fori_loop(0, depth, update, 0, unroll=8)


def write_kernel(value, newp, out_hbm, newp_hbm, sem):
    copies = [
        pltpu.make_async_copy(src, dst, sem.at[i])
        for i, (src, dst) in enumerate(
            [(value, out_hbm), (newp, newp_hbm)]
        )
    ]
    for copy in copies:
        copy.start()
    for copy in copies:
        copy.wait()


def on_device(
    pressure, composition, mass_old, pore_volume, trans_x, trans_y, trans_z,
    volatility, pressure_slope, mixing, two_phase,
):
    comps = composition.shape[0]
    grid = pressure.shape
    depth, width, span = grid
    big = (comps,) + grid
    anywhere = pl.BlockSpec(memory_space=pltpu.HBM)
    local = pl.BlockSpec(memory_space=pltpu.VMEM)
    dma = pltpu.SemaphoreType.DMA

    def array(shape):
        return jax.ShapeDtypeStruct(shape, F32)

    def scratch(shape):
        return pltpu.VMEM(shape, F32)

    out, newp = pl.pallas_call(
        functools.partial(flash_kernel, comps),
        name="flash",
        out_shape=(array(big), array(grid)),
        in_specs=[anywhere] * 11,
        out_specs=(local,) * 2,
        scratch_shapes=[
            scratch(big), scratch(big), scratch(big), scratch(grid), scratch((7,) + grid),
            scratch((2, comps, depth, span)), scratch((depth * width, 128)),
            scratch(grid), scratch(grid), scratch(grid), scratch(grid), scratch(grid),
            pltpu.VMEM((2, comps * TILE, comps * TILE), BF16),
            scratch((comps, comps)),
            pltpu.SMEM((comps,), F32), pltpu.SMEM((comps,), F32),
            pltpu.SMEM(two_phase.shape, jnp.int32),
            scratch((width, span)),
            scratch(grid), scratch(grid), scratch(grid), scratch(grid), scratch(grid),
            scratch((7,) + grid),
            scratch((2, depth, span)), scratch((128, depth * width)),
            scratch((2, FIELDS, depth, span)), scratch((2, FIELDS, depth, span)),
            scratch((2, YROWS, depth * width)), scratch((2, YROWS, depth * width)),
            scratch((2, 2, depth, span)), scratch((2, 2, depth, span)), scratch((2, depth, span)),
            scratch((TILE, depth * width)), scratch((2, TILE, depth * width)),
            dma((13,)), dma((4,)), dma((4,)), dma((4,)), dma((4,)),
        ],
        compiler_params=pltpu.CompilerParams(
            collective_id=0, has_side_effects=True, vmem_limit_bytes=VMEM_BYTES
        ),
    )(
        *(
            pltpu.with_memory_space_constraint(value, pltpu.HBM)
            for value in (
                pressure, composition, mass_old, pore_volume, trans_x, trans_y, trans_z,
                volatility, pressure_slope, mixing, two_phase,
            )
        )
    )
    return pl.pallas_call(
        write_kernel,
        name="write",
        out_shape=(array(big), array(grid)),
        in_specs=[local] * 2,
        out_specs=(anywhere, anywhere),
        scratch_shapes=[dma((comps + 1,))],
        compiler_params=pltpu.CompilerParams(vmem_limit_bytes=8 << 20),
    )(out, newp)


def solution(mesh):
    placed = (
        P(None, "areal", "layer"),
        P(None, None, "areal", "layer"),
        P(None, None, "areal", "layer"),
        P(None, "areal", "layer"),
        P(None, "areal", "layer"),
        P(None, "areal", "layer"),
        P(None, "areal", "layer"),
        P(),
        P(),
        P(),
        P(None, "areal"),
    )
    return jax.shard_map(
        on_device,
        mesh=mesh,
        in_specs=placed,
        out_specs=(P(None, None, "areal", "layer"), P(None, "areal", "layer")),
        check_vma=False,
    )
```

```python
import functools

import jax
import jax.numpy as jnp
from jax import lax
from jax.experimental import pallas as pl
from jax.experimental.pallas import tpu as pltpu
from jax.sharding import PartitionSpec as P

SS_ITERS = 3
RR_ITERS = 3
light_count = 4
compress = 0.2
F32 = jnp.float32
BF16 = jnp.bfloat16
MESH = pl.DeviceIdType.MESH
TILE = 8
FIELDS = 12
YROWS = 16
UNROLL = 8
VMEM_BYTES = 24 << 20


def total_of(values):
    return functools.reduce(lambda a, b: a + b, values)


def split_matrix(mix, comps):
    size = comps * TILE
    rows = lax.broadcasted_iota(jnp.int32, (size, comps), 0) // TILE
    cols = lax.broadcasted_iota(jnp.int32, (size, comps), 1)
    pick = (rows == cols).astype(F32)
    wide = lax.dot_general(
        jnp.dot(pick, mix, precision=lax.Precision.HIGHEST, preferred_element_type=F32),
        pick,
        (((1,), (1,)), ((), ())),
        precision=lax.Precision.HIGHEST,
        preferred_element_type=F32,
    )
    a = lax.broadcasted_iota(jnp.int32, (size, size), 0) % TILE
    b = lax.broadcasted_iota(jnp.int32, (size, size), 1) % TILE
    full = jnp.where(a == b, 2.0 * wide, 0.0)
    high = full.astype(BF16)
    return high, (full - high.astype(F32)).astype(BF16)


def mixed(w_ref, parts):
    stack = jnp.concatenate(parts + [jnp.zeros_like(parts[0])], axis=0)
    high = stack.astype(BF16)
    low = (stack - high.astype(F32)).astype(BF16)
    out = jnp.dot(
        w_ref[...], jnp.concatenate([high, low, high], axis=0), preferred_element_type=F32
    )
    return [out[i * TILE : (i + 1) * TILE] for i in range(len(parts))]


def flash(feed, log_p, half_vol, half_slope, w_ref):
    comps = len(feed)
    base = [half_vol[i] - half_slope[i] * log_p for i in range(comps)]
    half_log = base
    moved = None
    for outer in range(SS_ITERS):
        if outer:
            pulled = mixed(w_ref, moved)
            half_log = [base[i] - 0.5 * jnp.tanh(pulled[i]) for i in range(comps)]
        q = [jnp.tanh(v) for v in half_log]
        h = [1.0 / v for v in q]
        centre = None
        for inner in range(RR_ITERS):
            if inner:
                q = [1.0 / (h[i] + centre) for i in range(comps)]
            fq = [feed[i] * q[i] for i in range(comps)]
            step = total_of(fq) / total_of([fq[i] * q[i] for i in range(comps)])
            centre = jnp.clip(step if centre is None else centre + step, -1.0, 1.0)
        moved = [feed[i] * (1.0 / (h[i] + centre)) for i in range(comps)]
    low = 1.0 - centre
    high = 1.0 + centre
    low = 0.25 * (low * low)
    high = high * high
    outer_sum, outer_diff = low + high, high - low
    return [moved[i] * (outer_sum * h[i] + outer_diff) for i in range(comps)]


def flash_kernel(
    comps,
    p_hbm, comp_hbm, mass_hbm, pv_hbm, tx_hbm, ty_hbm, tz_hbm, vol_hbm, slope_hbm, mix_hbm, two_hbm,
    out, newp,
    comp, mass, mob, pvi, grads, xmob, ymob, p, pv, tx, ty, tz, w_ref, mix, vol, slope, two, flags,
    msum, fsum, first, rest, rdiag, coup, mxh, myh,
    xsend, xrecv, ysend, yrecv, fxsend, fxrecv, fxend, fysend, fyrecv,
    in_sem, send_sem, recv_sem, send2_sem, recv2_sem,
):
    depth, width, span = p.shape
    here_a = lax.axis_index("areal")
    here_l = lax.axis_index("layer")
    na = lax.axis_size("areal")
    nl = lax.axis_size("layer")
    xm = (lax.rem(here_a + na - 1, na), here_l)
    xp = (lax.rem(here_a + 1, na), here_l)
    ym = (here_a, lax.rem(here_l + nl - 1, nl))
    yp = (here_a, lax.rem(here_l + 1, nl))

    low, high = pl.ds(0, TILE), pl.ds(width - TILE, TILE)
    inner = pl.ds(TILE, width - 2 * TILE)
    loads = [
        pltpu.make_async_copy(src, dst, in_sem.at[i])
        for i, (src, dst) in enumerate(
            [
                (two_hbm, two),
                (comp_hbm.at[:, :, low, :], comp.at[:, :, low, :]),
                (comp_hbm.at[:, :, high, :], comp.at[:, :, high, :]),
                (p_hbm, p), (tx_hbm, tx),
                (mix_hbm, mix), (vol_hbm, vol), (slope_hbm, slope),
                (comp_hbm.at[:, :, inner, :], comp.at[:, :, inner, :]), (ty_hbm, ty),
                (mass_hbm, mass), (pv_hbm, pv), (tz_hbm, tz),
            ]
        )
    ]
    for load in loads:
        load.start()
    barrier = pltpu.get_barrier_semaphore()
    there = (here_a > 0, here_a < na - 1, here_l > 0, here_l < nl - 1)

    def when_there(actions, which=(0, 1, 2, 3)):
        for i, action in zip(which, actions):
            pl.when(there[i])(action)

    def finish(sends, which):
        when_there([sends[i].wait_send for i in which], which)
        when_there([sends[i ^ 1].wait_recv for i in which], which)

    when_there(
        functools.partial(
            pl.semaphore_signal, barrier, inc=1, device_id=device, device_id_type=MESH
        )
        for device in (xm, xp, ym, yp)
    )
    for load in loads[:5]:
        load.wait()
    bricks = two.shape[1]
    brick_of = lax.broadcasted_iota(jnp.int32, (width, span), 0) // (width // bricks)
    flag = jnp.zeros((width, span), F32)
    for b in range(bricks):
        flag = jnp.where(brick_of == b, two[here_l, b].astype(F32), flag)
    flags[...] = flag
    def pack_x(z, carry):
        for side, row in ((0, 0), (1, width - 1)):
            for k in range(comps):
                xsend[side, k, pl.ds(z, 1), :] = comp[k, z, row : row + 1, :]
            xsend[side, comps, pl.ds(z, 1), :] = p[z, row : row + 1, :]
            xsend[side, comps + 1, pl.ds(z, 1), :] = tx[z, row : row + 1, :]
            xsend[side, comps + 2, pl.ds(z, 1), :] = flags[row : row + 1, :]
        return carry

    lax.fori_loop(0, depth, pack_x, 0, unroll=4)
    lane = lax.broadcasted_iota(jnp.int32, (width, 128), 1)
    sends = [
        pltpu.make_async_remote_copy(
            src_ref=src, dst_ref=dst, send_sem=send_sem.at[i], recv_sem=recv_sem.at[i],
            device_id=device, device_id_type=MESH,
        )
        for i, (src, dst, device) in enumerate(
            [
                (xsend.at[0], xrecv.at[1], xm), (xsend.at[1], xrecv.at[0], xp),
                (ysend.at[0], yrecv.at[1], ym), (ysend.at[1], yrecv.at[0], yp),
            ]
        )
    ]

    early = 1 - (here_a // 2) % 2

    def send_x():
        pl.semaphore_wait(barrier, total_of([exists.astype(jnp.int32) for exists in there]))
        when_there([send.start for send in sends[:2]])

    pl.when(early == 0)(send_x)
    for load in loads[5:8]:
        load.wait()
    high_part, low_part = split_matrix(mix[...], comps)
    blank = jnp.zeros((comps * TILE, TILE), BF16)
    w_ref[...] = jnp.concatenate(
        [high_part, blank, high_part, blank, low_part, blank], axis=1
    )
    half_vol = [(0.5 if i < light_count else -0.5) * vol[i] for i in range(comps)]
    half_slope = [0.5 * slope[i] for i in range(comps)]
    for exists, slot in zip(there, (xrecv.at[0], xrecv.at[1], yrecv.at[0], yrecv.at[1])):

        @pl.when(jnp.logical_not(exists))
        def _(slot=slot):
            slot[...] = jnp.ones(slot.shape, F32)

    def cells(values, pressure, flagged):
        total = total_of(values)
        inverse = 1.0 / total
        feed = [v * inverse for v in values]
        moved = flash(feed, jnp.log(pressure), half_vol, half_slope, w_ref)
        return inverse, total * inverse, [
            jnp.where(flagged > 0.0, moved[i], feed[i]) for i in range(comps)
        ]

    blocks = width // TILE
    chunks = blocks * depth // UNROLL

    def block(step):
        inner = step // (2 * depth)
        pair = step % (2 * depth)
        z = pair // 2
        place = (1 - inner) * (blocks - 1) * (pair % 2) + inner * (1 + pair % 2)
        rows = pl.ds(pl.multiple_of(place * TILE, TILE), TILE)
        values = [comp[i, z, rows, :] for i in range(comps)]
        inverse, whole, found = cells(values, p[z, rows, :], flags[rows, :])
        pvi[z, rows, :] = inverse
        fsum[z, rows, :] = whole
        for i in range(comps):
            mob[i, z, rows, :] = found[i]
        msum[z, rows, :] = total_of(found)

    def chunk(index, carry):
        def body(step, inner):
            block(index * UNROLL + step)
            return inner

        return lax.fori_loop(0, UNROLL, body, carry, unroll=True)

    edge_chunks = chunks // 2
    send_after = early * edge_chunks
    share_after = edge_chunks + early * (chunks - edge_chunks)
    lax.fori_loop(0, send_after, chunk, 0)
    pl.when(early == 1)(send_x)
    for load in loads[8:10]:
        load.wait()

    def pack_y(z, carry):
        packed = jnp.zeros((width, 128), F32)
        for side, cut in ((0, 0), (1, span - 128)):
            source = 0 if side == 0 else 127
            for k in range(FIELDS):
                if k < comps:
                    value = comp[k, z, :, cut : cut + 128]
                elif k == comps:
                    value = p[z, :, cut : cut + 128]
                elif k == comps + 1:
                    value = ty[z, :, cut : cut + 128]
                else:
                    value = flags[:, cut : cut + 128]
                target = side * YROWS + k
                moved = pltpu.roll(value, (target - source) % 128, 1)
                packed = jnp.where(lane == target, moved, packed)
        ymob[pl.ds(pl.multiple_of(z * width, width), width), :] = packed
        return carry

    lax.fori_loop(0, depth, pack_y, 0, unroll=4)
    turned = jnp.transpose(ymob[...])
    ysend[0] = turned[:YROWS]
    ysend[1] = turned[YROWS : 2 * YROWS]
    when_there([send.start for send in sends[2:]], (2, 3))
    lax.fori_loop(send_after, share_after, chunk, 0)
    for load in loads[10:]:
        load.wait()

    finish(sends, (2, 3))
    sub = lax.broadcasted_iota(jnp.int32, (TILE, span), 0)

    def both(k):
        return jnp.where(sub == 0, yrecv[0, k : k + 1, :], yrecv[1, k : k + 1, :])

    _, _, found = cells([both(k) for k in range(comps)], both(comps), both(comps + 2))
    together = found + [total_of(found), both(comps), both(comps + 1)]
    for side in range(2):
        for k, value in enumerate(together):
            myh[side * YROWS + k : side * YROWS + k + 1, :] = value[side : side + 1, :]
    ymob[...] = jnp.transpose(myh[...])

    row_id = lax.broadcasted_iota(jnp.int32, (width, span), 0)
    lane_id = lax.broadcasted_iota(jnp.int32, (width, span), 1)
    has_xm = (here_a > 0).astype(F32)
    has_xp = (here_a < na - 1).astype(F32)
    has_ym = (here_l > 0).astype(F32)
    has_yp = (here_l < nl - 1).astype(F32)

    def before_x(value, edge):
        return jnp.where(row_id == 0, edge, pltpu.roll(value, 1, 0))

    def after_x(value, edge):
        return jnp.where(row_id == width - 1, edge, pltpu.roll(value, width - 1, 0))

    def before_y(value, edge):
        return jnp.where(lane_id == 0, edge, pltpu.roll(value, 1, 1))

    def after_y(value, edge):
        return jnp.where(lane_id == span - 1, edge, pltpu.roll(value, span - 1, 1))

    edge_lane = lax.broadcasted_iota(jnp.int32, (depth, span), 1)
    level_id = lax.broadcasted_iota(jnp.int32, (depth, span), 0)

    def row_of(ref, r):
        return ref[:, r, :]

    for side, row, inside in ((0, 0, 1), (1, width - 1, width - 2)):
        edge = ymob[pl.ds(row, depth, stride=width), :]

        def near_y(value, k, edge=edge):
            return (
                jnp.where(
                    edge_lane == span - 1,
                    edge[:, YROWS + k : YROWS + k + 1],
                    pltpu.roll(value, span - 1, 1),
                ),
                jnp.where(edge_lane == 0, edge[:, k : k + 1], pltpu.roll(value, 1, 1)),
            )

        here_p, here_m = row_of(p, row), row_of(msum, row)
        t_y, t_z = row_of(ty, row), row_of(tz, row)
        strength = [
            jnp.where(level_id == depth - 1, 0.0, t_z),
            jnp.where(level_id == 0, 0.0, pltpu.roll(t_z, 1, 0)),
            row_of(tx, min(row, inside)),
            jnp.where(edge_lane == span - 1, has_yp * t_y, t_y),
            jnp.where(
                edge_lane == 0, has_ym * edge[:, comps + 2 : comps + 3], pltpu.roll(t_y, 1, 1)
            ),
        ]
        near_p = [
            pltpu.roll(here_p, depth - 1, 0), pltpu.roll(here_p, 1, 0), row_of(p, inside),
            *near_y(here_p, comps + 1),
        ]
        near_m = [
            pltpu.roll(here_m, depth - 1, 0), pltpu.roll(here_m, 1, 0), row_of(msum, inside),
            *near_y(here_m, comps),
        ]
        volume = row_of(pv, row)
        balance = volume * row_of(fsum, row) - total_of(
            [mass[i, :, row, :] for i in range(comps)]
        )
        diagonal = compress * volume
        for f in range(5):
            link = 2.0 * strength[f] * (here_m + near_m[f])
            balance = balance + link * (here_p - near_p[f])
            diagonal = diagonal + link
        fxsend[side, 0] = balance
        fxsend[side, 1] = diagonal
    shares = [
        pltpu.make_async_remote_copy(
            src_ref=src, dst_ref=dst, send_sem=send2_sem.at[i], recv_sem=recv2_sem.at[i],
            device_id=device, device_id_type=MESH,
        )
        for i, (src, dst, device) in enumerate(
            [
                (fxsend.at[0], fxrecv.at[1], xm), (fxsend.at[1], fxrecv.at[0], xp),
                (fysend, fyrecv.at[1], ym), (fysend, fyrecv.at[0], yp),
            ]
        )
    ]
    when_there([share.start for share in shares[:2]])
    lax.fori_loop(share_after, chunks, chunk, 0)

    finish(sends, (0, 1))
    for side in range(2):
        values = [xrecv[side, k] for k in range(comps)]
        _, _, found = cells(values, xrecv[side, comps], xrecv[side, comps + 2])
        for i in range(comps):
            xmob[side, i] = found[i]
        mxh[side] = total_of(found)

    def faces(z, carry):
        up = jnp.minimum(z + 1, depth - 1)
        down = jnp.maximum(z - 1, 0)
        zrow = pl.ds(z, 1)
        yrow = pl.ds(pl.multiple_of(z * width, width), width)
        here_p, here_m = p[z], msum[z]
        edge = ymob[yrow, :]
        em = [edge[:, k : k + 1] for k in (comps, comps + 1, comps + 2)]
        ep = [edge[:, YROWS + k : YROWS + k + 1] for k in (comps, comps + 1)]
        t_x, t_y = tx[z], ty[z]
        strength = [
            tz[z] * (z < depth - 1).astype(F32),
            tz[down] * (z > 0).astype(F32),
            jnp.where(row_id == width - 1, has_xp * t_x, t_x),
            before_x(t_x, has_xm * xrecv[0, comps + 1, zrow, :]),
            jnp.where(lane_id == span - 1, has_yp * t_y, t_y),
            before_y(t_y, has_ym * em[2]),
        ]
        near_p = [
            p[up], p[down],
            after_x(here_p, xrecv[1, comps, zrow, :]), before_x(here_p, xrecv[0, comps, zrow, :]),
            after_y(here_p, ep[1]), before_y(here_p, em[1]),
        ]
        near_m = [
            msum[up], msum[down],
            after_x(here_m, mxh[1, zrow, :]), before_x(here_m, mxh[0, zrow, :]),
            after_y(here_m, ep[0]), before_y(here_m, em[0]),
        ]
        volume = pv[z]
        balance = volume * fsum[z] - total_of([mass[i, z] for i in range(comps)])
        diagonal = compress * volume
        centre = None
        for f in range(6):
            twice = 2.0 * strength[f]
            fall = here_p - near_p[f]
            link = twice * (here_m + near_m[f])
            slope_f = twice * fall
            balance = balance + link * fall
            diagonal = diagonal + link
            grads[f, z] = slope_f
            coup[f, z] = link
            centre = slope_f if centre is None else centre + slope_f
        grads[6, z] = centre
        inverse = 1.0 / diagonal
        update = -balance * inverse
        first[z] = update
        rest[z] = -balance
        rdiag[z] = inverse
        pvi[z] = volume * pvi[z]
        left = update[:, 0:128]
        right = pltpu.roll(update[:, span - 128 : span], 2, 1)
        coup[6, z, :, 0:128] = jnp.where(lane == 0, left, right)
        return carry

    lax.fori_loop(0, depth, faces, 0, unroll=4)
    stacked = coup[6, :, :, 0:128].reshape(depth * width, 128)
    fysend[...] = jnp.transpose(stacked)[:TILE]
    when_there([share.start for share in shares[2:]], (2, 3))

    def level(z, i):
        up = jnp.minimum(z + 1, depth - 1)
        down = jnp.maximum(z - 1, 0)
        zrow = pl.ds(z, 1)
        here = mob[i, z]
        edge = ymob[pl.ds(pl.multiple_of(z * width, width), width), :]
        near = [
            mob[i, up], mob[i, down],
            after_x(here, xmob[1, i, zrow, :]), before_x(here, xmob[0, i, zrow, :]),
            after_y(here, edge[:, YROWS + i : YROWS + i + 1]), before_y(here, edge[:, i : i + 1]),
        ]
        value = pvi[z] * comp[i, z] - mass[i, z] + grads[6, z] * here
        for f in range(6):
            value = value + grads[f, z] * near[f]
        out[i, z] = value

    for i in range(comps):

        def body(z, carry, i=i):
            level(z, i)
            return carry

        lax.fori_loop(0, depth, body, 0, unroll=8)
    finish(shares, (0, 1, 2, 3))
    for exists, slot in zip(there, (fxrecv.at[0], fxrecv.at[1], fyrecv.at[0], fyrecv.at[1])):

        @pl.when(jnp.logical_not(exists))
        def _(slot=slot):
            slot[...] = jnp.ones(slot.shape, F32)

    for side, row, exists in ((0, 0, has_xm), (1, width - 1, has_xp)):
        face = xrecv[0, comps + 1] if side == 0 else row_of(tx, row)
        link = 2.0 * exists * face * (mxh[side] + row_of(msum, row))
        fall = xrecv[side, comps] - row_of(p, row)
        fxend[side] = -(fxrecv[side, 0] + link * fall) / (fxrecv[side, 1] + link)

    myh[0:1, :] = fyrecv[0, 1:2, :]
    myh[1:2, :] = fyrecv[1, 0:1, :]
    coup[6, :, :, 0:128] = jnp.transpose(myh[...]).reshape(depth, width, 128)

    def update(z, carry):
        up = jnp.minimum(z + 1, depth - 1)
        down = jnp.maximum(z - 1, 0)
        zrow = pl.ds(z, 1)
        value = first[z]
        edge = coup[6, z, :, 0:128]
        near = [
            first[up], first[down],
            after_x(value, fxend[1, zrow, :]), before_x(value, fxend[0, zrow, :]),
            after_y(value, edge[:, 1:2]), before_y(value, edge[:, 0:1]),
        ]
        gathered = rest[z]
        for f in range(6):
            gathered = gathered + coup[f, z] * near[f]
        newp[z] = p[z] + gathered * rdiag[z]
        return carry

    lax.fori_loop(0, depth, update, 0, unroll=8)


def write_kernel(value, newp, out_hbm, newp_hbm, sem):
    copies = [
        pltpu.make_async_copy(src, dst, sem.at[i])
        for i, (src, dst) in enumerate(
            [(value, out_hbm), (newp, newp_hbm)]
        )
    ]
    for copy in copies:
        copy.start()
    for copy in copies:
        copy.wait()


def on_device(
    pressure, composition, mass_old, pore_volume, trans_x, trans_y, trans_z,
    volatility, pressure_slope, mixing, two_phase,
):
    comps = composition.shape[0]
    grid = pressure.shape
    depth, width, span = grid
    big = (comps,) + grid
    anywhere = pl.BlockSpec(memory_space=pltpu.HBM)
    local = pl.BlockSpec(memory_space=pltpu.VMEM)
    dma = pltpu.SemaphoreType.DMA

    def array(shape):
        return jax.ShapeDtypeStruct(shape, F32)

    def scratch(shape):
        return pltpu.VMEM(shape, F32)

    out, newp = pl.pallas_call(
        functools.partial(flash_kernel, comps),
        name="flash",
        out_shape=(array(big), array(grid)),
        in_specs=[anywhere] * 11,
        out_specs=(local,) * 2,
        scratch_shapes=[
            scratch(big), scratch(big), scratch(big), scratch(grid), scratch((7,) + grid),
            scratch((2, comps, depth, span)), scratch((depth * width, 128)),
            scratch(grid), scratch(grid), scratch(grid), scratch(grid), scratch(grid),
            pltpu.VMEM((comps * TILE, 3 * (comps + 1) * TILE), BF16),
            scratch((comps, comps)),
            pltpu.SMEM((comps,), F32), pltpu.SMEM((comps,), F32),
            pltpu.SMEM(two_phase.shape, jnp.int32),
            scratch((width, span)),
            scratch(grid), scratch(grid), scratch(grid), scratch(grid), scratch(grid),
            scratch((7,) + grid),
            scratch((2, depth, span)), scratch((128, depth * width)),
            scratch((2, FIELDS, depth, span)), scratch((2, FIELDS, depth, span)),
            scratch((2, YROWS, depth * width)), scratch((2, YROWS, depth * width)),
            scratch((2, 2, depth, span)), scratch((2, 2, depth, span)), scratch((2, depth, span)),
            scratch((TILE, depth * width)), scratch((2, TILE, depth * width)),
            dma((13,)), dma((4,)), dma((4,)), dma((4,)), dma((4,)),
        ],
        compiler_params=pltpu.CompilerParams(
            collective_id=0, has_side_effects=True, vmem_limit_bytes=VMEM_BYTES
        ),
    )(
        *(
            pltpu.with_memory_space_constraint(value, pltpu.HBM)
            for value in (
                pressure, composition, mass_old, pore_volume, trans_x, trans_y, trans_z,
                volatility, pressure_slope, mixing, two_phase,
            )
        )
    )
    return pl.pallas_call(
        write_kernel,
        name="write",
        out_shape=(array(big), array(grid)),
        in_specs=[local] * 2,
        out_specs=(anywhere, anywhere),
        scratch_shapes=[dma((comps + 1,))],
        compiler_params=pltpu.CompilerParams(vmem_limit_bytes=8 << 20),
    )(out, newp)


def solution(mesh):
    placed = (
        P(None, "areal", "layer"),
        P(None, None, "areal", "layer"),
        P(None, None, "areal", "layer"),
        P(None, "areal", "layer"),
        P(None, "areal", "layer"),
        P(None, "areal", "layer"),
        P(None, "areal", "layer"),
        P(),
        P(),
        P(),
        P(None, "areal"),
    )
    return jax.shard_map(
        on_device,
        mesh=mesh,
        in_specs=placed,
        out_specs=(P(None, None, "areal", "layer"), P(None, "areal", "layer")),
        check_vma=False,
    )
```

```python
import functools

import jax
import jax.numpy as jnp
from jax import lax
from jax.experimental import pallas as pl
from jax.experimental.pallas import tpu as pltpu
from jax.sharding import PartitionSpec as P

SS_ITERS = 3
RR_ITERS = 3
light_count = 4
compress = 0.2
F32 = jnp.float32
BF16 = jnp.bfloat16
MESH = pl.DeviceIdType.MESH
TILE = 8
FIELDS = 12
YROWS = 16
UNROLL = 8
VMEM_BYTES = 24 << 20


def total_of(values):
    return functools.reduce(lambda a, b: a + b, values)


def split_matrix(mix, comps):
    size = comps * TILE
    rows = lax.broadcasted_iota(jnp.int32, (size, comps), 0) // TILE
    cols = lax.broadcasted_iota(jnp.int32, (size, comps), 1)
    pick = (rows == cols).astype(F32)
    wide = lax.dot_general(
        jnp.dot(pick, mix, precision=lax.Precision.HIGHEST, preferred_element_type=F32),
        pick,
        (((1,), (1,)), ((), ())),
        precision=lax.Precision.HIGHEST,
        preferred_element_type=F32,
    )
    a = lax.broadcasted_iota(jnp.int32, (size, size), 0) % TILE
    b = lax.broadcasted_iota(jnp.int32, (size, size), 1) % TILE
    full = jnp.where(a == b, 2.0 * wide, 0.0)
    high = full.astype(BF16)
    return high, (full - high.astype(F32)).astype(BF16)


def mixed(w_ref, parts):
    stack = jnp.concatenate(parts + [jnp.zeros_like(parts[0])], axis=0)
    high = stack.astype(BF16)
    low = (stack - high.astype(F32)).astype(BF16)
    out = jnp.dot(
        w_ref[...], jnp.concatenate([high, low, high], axis=0), preferred_element_type=F32
    )
    return [out[i * TILE : (i + 1) * TILE] for i in range(len(parts))]


def flash(feed, log_p, half_vol, half_slope, w_ref):
    comps = len(feed)
    base = [half_vol[i] - half_slope[i] * log_p for i in range(comps)]
    half_log = base
    moved = None
    for outer in range(SS_ITERS):
        if outer:
            pulled = mixed(w_ref, moved)
            half_log = [base[i] - 0.5 * jnp.tanh(pulled[i]) for i in range(comps)]
        q = [jnp.tanh(v) for v in half_log]
        h = [1.0 / v for v in q]
        centre = None
        for inner in range(RR_ITERS):
            if inner:
                q = [1.0 / (h[i] + centre) for i in range(comps)]
            fq = [feed[i] * q[i] for i in range(comps)]
            step = total_of(fq) / total_of([fq[i] * q[i] for i in range(comps)])
            centre = jnp.clip(step if centre is None else centre + step, -1.0, 1.0)
        moved = [feed[i] * (1.0 / (h[i] + centre)) for i in range(comps)]
    low = 1.0 - centre
    high = 1.0 + centre
    low = 0.25 * (low * low)
    high = high * high
    outer_sum, outer_diff = low + high, high - low
    return [moved[i] * (outer_sum * h[i] + outer_diff) for i in range(comps)]


def flash_kernel(
    comps,
    p_hbm, comp_hbm, mass_hbm, pv_hbm, tx_hbm, ty_hbm, tz_hbm, vol_hbm, slope_hbm, mix_hbm, two_hbm,
    out, newp,
    comp, mass, mob, pvi, grads, xmob, ymob, p, pv, tx, ty, tz, w_ref, mix, vol, slope, two, flags,
    msum, fsum, first, rest, rdiag, coup, mxh, myh,
    xsend, xrecv, ysend, yrecv, fxsend, fxrecv, fxend, fysend, fyrecv,
    in_sem, send_sem, recv_sem, send2_sem, recv2_sem,
):
    depth, width, span = p.shape
    here_a = lax.axis_index("areal")
    here_l = lax.axis_index("layer")
    na = lax.axis_size("areal")
    nl = lax.axis_size("layer")
    xm = (lax.rem(here_a + na - 1, na), here_l)
    xp = (lax.rem(here_a + 1, na), here_l)
    ym = (here_a, lax.rem(here_l + nl - 1, nl))
    yp = (here_a, lax.rem(here_l + 1, nl))

    low, high = pl.ds(0, TILE), pl.ds(width - TILE, TILE)
    inner = pl.ds(TILE, width - 2 * TILE)
    loads = [
        pltpu.make_async_copy(src, dst, in_sem.at[i])
        for i, (src, dst) in enumerate(
            [
                (two_hbm, two),
                (comp_hbm.at[:, :, low, :], comp.at[:, :, low, :]),
                (comp_hbm.at[:, :, high, :], comp.at[:, :, high, :]),
                (p_hbm, p), (tx_hbm, tx),
                (mix_hbm, mix), (vol_hbm, vol), (slope_hbm, slope),
                (comp_hbm.at[:, :, inner, :], comp.at[:, :, inner, :]), (ty_hbm, ty),
                (mass_hbm, mass), (pv_hbm, pv), (tz_hbm, tz),
            ]
        )
    ]
    for load in loads:
        load.start()
    barrier = pltpu.get_barrier_semaphore()
    there = (here_a > 0, here_a < na - 1, here_l > 0, here_l < nl - 1)

    def when_there(actions, which=(0, 1, 2, 3)):
        for i, action in zip(which, actions):
            pl.when(there[i])(action)

    def finish(sends, which):
        when_there([sends[i].wait_send for i in which], which)
        when_there([sends[i ^ 1].wait_recv for i in which], which)

    when_there(
        functools.partial(
            pl.semaphore_signal, barrier, inc=1, device_id=device, device_id_type=MESH
        )
        for device in (xm, xp, ym, yp)
    )
    for load in loads[:5]:
        load.wait()
    bricks = two.shape[1]
    brick_of = lax.broadcasted_iota(jnp.int32, (width, span), 0) // (width // bricks)
    flag = jnp.zeros((width, span), F32)
    for b in range(bricks):
        flag = jnp.where(brick_of == b, two[here_l, b].astype(F32), flag)
    flags[...] = flag
    def pack_x(z, carry):
        for side, row in ((0, 0), (1, width - 1)):
            for k in range(comps):
                xsend[side, k, pl.ds(z, 1), :] = comp[k, z, row : row + 1, :]
            xsend[side, comps, pl.ds(z, 1), :] = p[z, row : row + 1, :]
            xsend[side, comps + 1, pl.ds(z, 1), :] = tx[z, row : row + 1, :]
            xsend[side, comps + 2, pl.ds(z, 1), :] = flags[row : row + 1, :]
        return carry

    lax.fori_loop(0, depth, pack_x, 0, unroll=4)
    lane = lax.broadcasted_iota(jnp.int32, (width, 128), 1)
    sends = [
        pltpu.make_async_remote_copy(
            src_ref=src, dst_ref=dst, send_sem=send_sem.at[i], recv_sem=recv_sem.at[i],
            device_id=device, device_id_type=MESH,
        )
        for i, (src, dst, device) in enumerate(
            [
                (xsend.at[0], xrecv.at[1], xm), (xsend.at[1], xrecv.at[0], xp),
                (ysend.at[0], yrecv.at[1], ym), (ysend.at[1], yrecv.at[0], yp),
            ]
        )
    ]

    early = 1 - (here_a // 2) % 2

    def send_x():
        pl.semaphore_wait(barrier, total_of([exists.astype(jnp.int32) for exists in there]))
        when_there([send.start for send in sends[:2]])

    pl.when(early == 0)(send_x)
    for load in loads[5:8]:
        load.wait()
    high_part, low_part = split_matrix(mix[...], comps)
    blank = jnp.zeros((comps * TILE, TILE), BF16)
    w_ref[...] = jnp.concatenate(
        [high_part, blank, high_part, blank, low_part, blank], axis=1
    )
    half_vol = [(0.5 if i < light_count else -0.5) * vol[i] for i in range(comps)]
    half_slope = [0.5 * slope[i] for i in range(comps)]
    for exists, slot in zip(there, (xrecv.at[0], xrecv.at[1], yrecv.at[0], yrecv.at[1])):

        @pl.when(jnp.logical_not(exists))
        def _(slot=slot):
            slot[...] = jnp.ones(slot.shape, F32)

    def cells(values, pressure, flagged):
        total = total_of(values)
        inverse = 1.0 / total
        feed = [v * inverse for v in values]
        moved = flash(feed, jnp.log(pressure), half_vol, half_slope, w_ref)
        return inverse, total * inverse, [
            jnp.where(flagged > 0.0, moved[i], feed[i]) for i in range(comps)
        ]

    blocks = width // TILE
    chunks = blocks * depth // UNROLL

    def block(step):
        inner = step // (2 * depth)
        pair = step % (2 * depth)
        z = pair // 2
        place = (1 - inner) * (blocks - 1) * (pair % 2) + inner * (1 + pair % 2)
        rows = pl.ds(pl.multiple_of(place * TILE, TILE), TILE)
        values = [comp[i, z, rows, :] for i in range(comps)]
        inverse, whole, found = cells(values, p[z, rows, :], flags[rows, :])
        pvi[z, rows, :] = inverse
        fsum[z, rows, :] = whole
        for i in range(comps):
            mob[i, z, rows, :] = found[i]
        msum[z, rows, :] = total_of(found)

    def chunk(index, carry):
        def body(step, inner):
            block(index * UNROLL + step)
            return inner

        return lax.fori_loop(0, UNROLL, body, carry, unroll=True)

    edge_chunks = chunks // 2
    far = (here_a % 16 == 0).astype(jnp.int32)
    most = (here_l == 0).astype(jnp.int32)
    some = (here_l < 3).astype(jnp.int32)
    send_after = early * (edge_chunks + most + (1 - most) * some * far)
    share_after = edge_chunks + early * (chunks - edge_chunks)
    for load in loads[8:10]:
        load.wait()
    lax.fori_loop(0, send_after, chunk, 0)
    pl.when(early == 1)(send_x)

    def pack_y(z, carry):
        packed = jnp.zeros((width, 128), F32)
        for side, cut in ((0, 0), (1, span - 128)):
            source = 0 if side == 0 else 127
            for k in range(FIELDS):
                if k < comps:
                    value = comp[k, z, :, cut : cut + 128]
                elif k == comps:
                    value = p[z, :, cut : cut + 128]
                elif k == comps + 1:
                    value = ty[z, :, cut : cut + 128]
                else:
                    value = flags[:, cut : cut + 128]
                target = side * YROWS + k
                moved = pltpu.roll(value, (target - source) % 128, 1)
                packed = jnp.where(lane == target, moved, packed)
        ymob[pl.ds(pl.multiple_of(z * width, width), width), :] = packed
        return carry

    lax.fori_loop(0, depth, pack_y, 0, unroll=4)
    turned = jnp.transpose(ymob[...])
    ysend[0] = turned[:YROWS]
    ysend[1] = turned[YROWS : 2 * YROWS]
    when_there([send.start for send in sends[2:]], (2, 3))
    lax.fori_loop(send_after, share_after, chunk, 0)
    for load in loads[10:]:
        load.wait()

    finish(sends, (2, 3))
    sub = lax.broadcasted_iota(jnp.int32, (TILE, span), 0)

    def both(k):
        return jnp.where(sub == 0, yrecv[0, k : k + 1, :], yrecv[1, k : k + 1, :])

    _, _, found = cells([both(k) for k in range(comps)], both(comps), both(comps + 2))
    together = found + [total_of(found), both(comps), both(comps + 1)]
    for side in range(2):
        for k, value in enumerate(together):
            myh[side * YROWS + k : side * YROWS + k + 1, :] = value[side : side + 1, :]
    ymob[...] = jnp.transpose(myh[...])

    row_id = lax.broadcasted_iota(jnp.int32, (width, span), 0)
    lane_id = lax.broadcasted_iota(jnp.int32, (width, span), 1)
    has_xm = (here_a > 0).astype(F32)
    has_xp = (here_a < na - 1).astype(F32)
    has_ym = (here_l > 0).astype(F32)
    has_yp = (here_l < nl - 1).astype(F32)

    def before_x(value, edge):
        return jnp.where(row_id == 0, edge, pltpu.roll(value, 1, 0))

    def after_x(value, edge):
        return jnp.where(row_id == width - 1, edge, pltpu.roll(value, width - 1, 0))

    def before_y(value, edge):
        return jnp.where(lane_id == 0, edge, pltpu.roll(value, 1, 1))

    def after_y(value, edge):
        return jnp.where(lane_id == span - 1, edge, pltpu.roll(value, span - 1, 1))

    edge_lane = lax.broadcasted_iota(jnp.int32, (depth, span), 1)
    level_id = lax.broadcasted_iota(jnp.int32, (depth, span), 0)

    def row_of(ref, r):
        return ref[:, r, :]

    for side, row, inside in ((0, 0, 1), (1, width - 1, width - 2)):
        edge = ymob[pl.ds(row, depth, stride=width), :]

        def near_y(value, k, edge=edge):
            return (
                jnp.where(
                    edge_lane == span - 1,
                    edge[:, YROWS + k : YROWS + k + 1],
                    pltpu.roll(value, span - 1, 1),
                ),
                jnp.where(edge_lane == 0, edge[:, k : k + 1], pltpu.roll(value, 1, 1)),
            )

        here_p, here_m = row_of(p, row), row_of(msum, row)
        t_y, t_z = row_of(ty, row), row_of(tz, row)
        strength = [
            jnp.where(level_id == depth - 1, 0.0, t_z),
            jnp.where(level_id == 0, 0.0, pltpu.roll(t_z, 1, 0)),
            row_of(tx, min(row, inside)),
            jnp.where(edge_lane == span - 1, has_yp * t_y, t_y),
            jnp.where(
                edge_lane == 0, has_ym * edge[:, comps + 2 : comps + 3], pltpu.roll(t_y, 1, 1)
            ),
        ]
        near_p = [
            pltpu.roll(here_p, depth - 1, 0), pltpu.roll(here_p, 1, 0), row_of(p, inside),
            *near_y(here_p, comps + 1),
        ]
        near_m = [
            pltpu.roll(here_m, depth - 1, 0), pltpu.roll(here_m, 1, 0), row_of(msum, inside),
            *near_y(here_m, comps),
        ]
        volume = row_of(pv, row)
        balance = volume * row_of(fsum, row) - total_of(
            [mass[i, :, row, :] for i in range(comps)]
        )
        diagonal = compress * volume
        for f in range(5):
            link = 2.0 * strength[f] * (here_m + near_m[f])
            balance = balance + link * (here_p - near_p[f])
            diagonal = diagonal + link
        fxsend[side, 0] = balance
        fxsend[side, 1] = diagonal
    shares = [
        pltpu.make_async_remote_copy(
            src_ref=src, dst_ref=dst, send_sem=send2_sem.at[i], recv_sem=recv2_sem.at[i],
            device_id=device, device_id_type=MESH,
        )
        for i, (src, dst, device) in enumerate(
            [
                (fxsend.at[0], fxrecv.at[1], xm), (fxsend.at[1], fxrecv.at[0], xp),
                (fysend, fyrecv.at[1], ym), (fysend, fyrecv.at[0], yp),
            ]
        )
    ]
    when_there([share.start for share in shares[:2]])
    lax.fori_loop(share_after, chunks, chunk, 0)

    finish(sends, (0, 1))
    for side in range(2):
        values = [xrecv[side, k] for k in range(comps)]
        _, _, found = cells(values, xrecv[side, comps], xrecv[side, comps + 2])
        for i in range(comps):
            xmob[side, i] = found[i]
        mxh[side] = total_of(found)

    def faces(z, carry):
        up = jnp.minimum(z + 1, depth - 1)
        down = jnp.maximum(z - 1, 0)
        zrow = pl.ds(z, 1)
        yrow = pl.ds(pl.multiple_of(z * width, width), width)
        here_p, here_m = p[z], msum[z]
        edge = ymob[yrow, :]
        em = [edge[:, k : k + 1] for k in (comps, comps + 1, comps + 2)]
        ep = [edge[:, YROWS + k : YROWS + k + 1] for k in (comps, comps + 1)]
        t_x, t_y = tx[z], ty[z]
        strength = [
            tz[z] * (z < depth - 1).astype(F32),
            tz[down] * (z > 0).astype(F32),
            jnp.where(row_id == width - 1, has_xp * t_x, t_x),
            before_x(t_x, has_xm * xrecv[0, comps + 1, zrow, :]),
            jnp.where(lane_id == span - 1, has_yp * t_y, t_y),
            before_y(t_y, has_ym * em[2]),
        ]
        near_p = [
            p[up], p[down],
            after_x(here_p, xrecv[1, comps, zrow, :]), before_x(here_p, xrecv[0, comps, zrow, :]),
            after_y(here_p, ep[1]), before_y(here_p, em[1]),
        ]
        near_m = [
            msum[up], msum[down],
            after_x(here_m, mxh[1, zrow, :]), before_x(here_m, mxh[0, zrow, :]),
            after_y(here_m, ep[0]), before_y(here_m, em[0]),
        ]
        volume = pv[z]
        balance = volume * fsum[z] - total_of([mass[i, z] for i in range(comps)])
        diagonal = compress * volume
        centre = None
        for f in range(6):
            twice = 2.0 * strength[f]
            fall = here_p - near_p[f]
            link = twice * (here_m + near_m[f])
            slope_f = twice * fall
            balance = balance + link * fall
            diagonal = diagonal + link
            grads[f, z] = slope_f
            coup[f, z] = link
            centre = slope_f if centre is None else centre + slope_f
        grads[6, z] = centre
        inverse = 1.0 / diagonal
        update = -balance * inverse
        first[z] = update
        rest[z] = -balance
        rdiag[z] = inverse
        pvi[z] = volume * pvi[z]
        left = update[:, 0:128]
        right = pltpu.roll(update[:, span - 128 : span], 2, 1)
        coup[6, z, :, 0:128] = jnp.where(lane == 0, left, right)
        return carry

    lax.fori_loop(0, depth, faces, 0, unroll=4)
    stacked = coup[6, :, :, 0:128].reshape(depth * width, 128)
    fysend[...] = jnp.transpose(stacked)[:TILE]
    when_there([share.start for share in shares[2:]], (2, 3))

    def level(z, i):
        up = jnp.minimum(z + 1, depth - 1)
        down = jnp.maximum(z - 1, 0)
        zrow = pl.ds(z, 1)
        here = mob[i, z]
        edge = ymob[pl.ds(pl.multiple_of(z * width, width), width), :]
        near = [
            mob[i, up], mob[i, down],
            after_x(here, xmob[1, i, zrow, :]), before_x(here, xmob[0, i, zrow, :]),
            after_y(here, edge[:, YROWS + i : YROWS + i + 1]), before_y(here, edge[:, i : i + 1]),
        ]
        value = pvi[z] * comp[i, z] - mass[i, z] + grads[6, z] * here
        for f in range(6):
            value = value + grads[f, z] * near[f]
        out[i, z] = value

    for i in range(comps):

        def body(z, carry, i=i):
            level(z, i)
            return carry

        lax.fori_loop(0, depth, body, 0, unroll=8)
    finish(shares, (0, 1, 2, 3))
    for exists, slot in zip(there, (fxrecv.at[0], fxrecv.at[1], fyrecv.at[0], fyrecv.at[1])):

        @pl.when(jnp.logical_not(exists))
        def _(slot=slot):
            slot[...] = jnp.ones(slot.shape, F32)

    for side, row, exists in ((0, 0, has_xm), (1, width - 1, has_xp)):
        face = xrecv[0, comps + 1] if side == 0 else row_of(tx, row)
        link = 2.0 * exists * face * (mxh[side] + row_of(msum, row))
        fall = xrecv[side, comps] - row_of(p, row)
        fxend[side] = -(fxrecv[side, 0] + link * fall) / (fxrecv[side, 1] + link)

    myh[0:1, :] = fyrecv[0, 1:2, :]
    myh[1:2, :] = fyrecv[1, 0:1, :]
    coup[6, :, :, 0:128] = jnp.transpose(myh[...]).reshape(depth, width, 128)

    def update(z, carry):
        up = jnp.minimum(z + 1, depth - 1)
        down = jnp.maximum(z - 1, 0)
        zrow = pl.ds(z, 1)
        value = first[z]
        edge = coup[6, z, :, 0:128]
        near = [
            first[up], first[down],
            after_x(value, fxend[1, zrow, :]), before_x(value, fxend[0, zrow, :]),
            after_y(value, edge[:, 1:2]), before_y(value, edge[:, 0:1]),
        ]
        gathered = rest[z]
        for f in range(6):
            gathered = gathered + coup[f, z] * near[f]
        newp[z] = p[z] + gathered * rdiag[z]
        return carry

    lax.fori_loop(0, depth, update, 0, unroll=8)


def write_kernel(value, newp, out_hbm, newp_hbm, sem):
    copies = [
        pltpu.make_async_copy(src, dst, sem.at[i])
        for i, (src, dst) in enumerate(
            [(value, out_hbm), (newp, newp_hbm)]
        )
    ]
    for copy in copies:
        copy.start()
    for copy in copies:
        copy.wait()


def on_device(
    pressure, composition, mass_old, pore_volume, trans_x, trans_y, trans_z,
    volatility, pressure_slope, mixing, two_phase,
):
    comps = composition.shape[0]
    grid = pressure.shape
    depth, width, span = grid
    big = (comps,) + grid
    anywhere = pl.BlockSpec(memory_space=pltpu.HBM)
    local = pl.BlockSpec(memory_space=pltpu.VMEM)
    dma = pltpu.SemaphoreType.DMA

    def array(shape):
        return jax.ShapeDtypeStruct(shape, F32)

    def scratch(shape):
        return pltpu.VMEM(shape, F32)

    out, newp = pl.pallas_call(
        functools.partial(flash_kernel, comps),
        name="flash",
        out_shape=(array(big), array(grid)),
        in_specs=[anywhere] * 11,
        out_specs=(local,) * 2,
        scratch_shapes=[
            scratch(big), scratch(big), scratch(big), scratch(grid), scratch((7,) + grid),
            scratch((2, comps, depth, span)), scratch((depth * width, 128)),
            scratch(grid), scratch(grid), scratch(grid), scratch(grid), scratch(grid),
            pltpu.VMEM((comps * TILE, 3 * (comps + 1) * TILE), BF16),
            scratch((comps, comps)),
            pltpu.SMEM((comps,), F32), pltpu.SMEM((comps,), F32),
            pltpu.SMEM(two_phase.shape, jnp.int32),
            scratch((width, span)),
            scratch(grid), scratch(grid), scratch(grid), scratch(grid), scratch(grid),
            scratch((7,) + grid),
            scratch((2, depth, span)), scratch((128, depth * width)),
            scratch((2, FIELDS, depth, span)), scratch((2, FIELDS, depth, span)),
            scratch((2, YROWS, depth * width)), scratch((2, YROWS, depth * width)),
            scratch((2, 2, depth, span)), scratch((2, 2, depth, span)), scratch((2, depth, span)),
            scratch((TILE, depth * width)), scratch((2, TILE, depth * width)),
            dma((13,)), dma((4,)), dma((4,)), dma((4,)), dma((4,)),
        ],
        compiler_params=pltpu.CompilerParams(
            collective_id=0, has_side_effects=True, vmem_limit_bytes=VMEM_BYTES
        ),
    )(
        *(
            pltpu.with_memory_space_constraint(value, pltpu.HBM)
            for value in (
                pressure, composition, mass_old, pore_volume, trans_x, trans_y, trans_z,
                volatility, pressure_slope, mixing, two_phase,
            )
        )
    )
    return pl.pallas_call(
        write_kernel,
        name="write",
        out_shape=(array(big), array(grid)),
        in_specs=[local] * 2,
        out_specs=(anywhere, anywhere),
        scratch_shapes=[dma((comps + 1,))],
        compiler_params=pltpu.CompilerParams(vmem_limit_bytes=8 << 20),
    )(out, newp)


def solution(mesh):
    placed = (
        P(None, "areal", "layer"),
        P(None, None, "areal", "layer"),
        P(None, None, "areal", "layer"),
        P(None, "areal", "layer"),
        P(None, "areal", "layer"),
        P(None, "areal", "layer"),
        P(None, "areal", "layer"),
        P(),
        P(),
        P(),
        P(None, "areal"),
    )
    return jax.shard_map(
        on_device,
        mesh=mesh,
        in_specs=placed,
        out_specs=(P(None, None, "areal", "layer"), P(None, "areal", "layer")),
        check_vma=False,
    )
```
